32 devices in a mesh: view: 8 (over z, core), strip: 2 (over x), orbit: 2 (over y).
Axes of the slice: x: 2, y: 2, z: 4, core: 2. Of those that a mesh axis runs over, the one named last changes fastest.
Arguments:
- features: bfloat16 [16, 8, 128, 256], P(('orbit', 'view'), 'strip'), parts along dimension 0, may hold values from -6 to 6
- cotangent: bfloat16 [16, 8, 128, 256], P(('orbit', 'view'), 'strip'), parts along dimension 0, may hold values from -6 to 6
- conv_first: bfloat16 [3, 3, 256, 256], replicated, may hold values from -0.125 to 0.125
- conv_second: bfloat16 [3, 3, 256, 256], replicated, may hold values from -0.125 to 0.125
- w_query: bfloat16 [256, 256], replicated, may hold values from -6 to 6
- w_key: bfloat16 [256, 256], replicated, may hold values from -6 to 6
- w_value: bfloat16 [256, 256], replicated, may hold values from -0.375 to 0.375
- w_out: bfloat16 [256, 256], replicated, may hold values from -0.375 to 0.375
Outputs:
- grad_features: bfloat16 [16, 8, 128, 256], P(('orbit', 'view'), 'strip'), parts along dimension 0
- conv_grads: float32 [4, 2304, 256], P('orbit', 'view'), parts along dimension 0
- attn_grads: float32 [8, 256, 256], P('orbit', 'view'), parts along dimension 0
The draws below stay inside these ranges and needn't reach their ends.
There are 2 independent parts, one for each index of `orbit`. The reference program is written for one: setup_inputs(seed, part) draws one part's arguments, and reference() takes and returns one part's arrays. A program takes and returns all parts, laid end to end along the dimension named above; an argument that names none is the same for every part. Nothing has to cross between parts.
All inputs are finite; a program needn't handle non-finite values.
Results may differ from the reference program's by a relative error of at most 0.017.
Values may be sent and summed in bfloat16 or wider, within the bound.
A program may use at most 64 MiB of HBM per device.

```python
import jax
import jax.numpy as jnp
from jax import lax

C = 256
COLS = 128
ROWS = 8
VIEWS = 8


def attention_pair(key):
    base = jax.random.fold_in(key, 4242)
    keys = jax.random.split(base, 3)
    scale = C ** (-0.5)
    noise_query = jnp.clip(jax.random.normal(keys[1], (C, C), jnp.float32), -6.0, 6.0)
    noise_key = jnp.clip(jax.random.normal(keys[2], (C, C), jnp.float32), -6.0, 6.0)
    first = scale * noise_query
    second = scale * noise_key
    return (first, second)


def draw_w_query(key, part):
    return attention_pair(key)[0].astype(jnp.bfloat16)


def draw_w_key(key, part):
    return attention_pair(key)[1].astype(jnp.bfloat16)


def shard_levels(stream_key, dims, cuts, least, top_value):
    loudness, own = 1.0, jax.random.fold_in(stream_key, 6)
    for dim, blocks in cuts:
        steps = jnp.exp(jax.random.uniform(jax.random.fold_in(own, dim), (blocks,), jnp.float32, least / len(cuts), top_value / len(cuts)))
        loudness = loudness * jnp.repeat(steps, dims[dim] // blocks).reshape([-1 if axis == dim else 1 for axis in range(len(dims))])
    return loudness


def bell_draw(key, shape, scale, bound, cuts=(), dtype=jnp.bfloat16):
    drawn = jax.random.normal(key, shape, jnp.float32) * scale
    if len(cuts) > 0:
        drawn = shard_levels(key, shape, cuts, -0.22, 0.18) * drawn
    return jnp.clip(drawn, min=-bound, max=bound).astype(dtype)


def setup_inputs(seed: int = 0, part: int = 0) -> dict:
    arg_keys = jax.random.split(jax.random.key(seed), 9)
    part_keys = jax.random.split(jax.random.fold_in(arg_keys[8], part), 9)
    return {
        "features": bell_draw(part_keys[0], (VIEWS, ROWS, COLS, C), 1.0, 6.0, ((0, 8), (1, 2))),
        "cotangent": bell_draw(part_keys[1], (VIEWS, ROWS, COLS, C), 1.0, 6.0, ((0, 8), (1, 2))),
        "conv_first": bell_draw(arg_keys[2], (3, 3, C, C), (9 * C) ** -0.5, 0.125),
        "conv_second": bell_draw(arg_keys[3], (3, 3, C, C), (9 * C) ** -0.5, 0.125),
        "w_query": draw_w_query(jax.random.fold_in(arg_keys[8], 71), part),
        "w_key": draw_w_key(jax.random.fold_in(arg_keys[8], 71), part),
        "w_value": bell_draw(arg_keys[6], (C, C), C ** -0.5, 0.375),
        "w_out": bell_draw(arg_keys[7], (C, C), C ** -0.5, 0.375),
    }


def rounded(array):
    return lax.optimization_barrier(array.astype(jnp.bfloat16))

def silu_slope(value):
    sigma = jax.nn.sigmoid(value)
    return sigma * (1.0 + value * (1.0 - sigma))

def pad_cells(array):
    return jnp.pad(array, ((0, 0), (1, 1), (1, 1), (0, 0)))

def flipped(kernel):
    return jnp.transpose(kernel[::-1, ::-1], (0, 1, 3, 2))

def convolve(padded, kernel):
    lead = padded.shape[0]
    rows = padded.shape[1] - 2
    cols = padded.shape[2] - 2
    chan = padded.shape[3]
    total = jnp.zeros((lead * rows * cols, kernel.shape[3]), jnp.float32)
    for shift_row in range(3):
        for shift_col in range(3):
            piece = padded[:, shift_row:shift_row + rows, shift_col:shift_col + cols, :].reshape(-1, chan)
            total = total + jnp.dot(piece.astype(jnp.float32), kernel[shift_row, shift_col].astype(jnp.float32))
    return total.reshape(lead, rows, cols, -1)

def kernel_grad(padded, upstream):
    rows = padded.shape[1] - 2
    cols = padded.shape[2] - 2
    chan = padded.shape[3]
    flat_up = upstream.reshape(-1, upstream.shape[3]).astype(jnp.float32)
    pieces = []
    for shift_row in range(3):
        for shift_col in range(3):
            piece = padded[:, shift_row:shift_row + rows, shift_col:shift_col + cols, :].reshape(-1, chan)
            pieces.append(lax.dot_general(piece.astype(jnp.float32), flat_up, (((0,), (0,)), ((), ()))))
    return jnp.stack(pieces).reshape(9 * chan, -1)

def attend(query, key, value, grad_mixed):
    chan = query.shape[-1]
    scale = chan ** (-0.5)
    query_f = query.astype(jnp.float32)
    key_f = key.astype(jnp.float32)
    value_f = value.astype(jnp.float32)
    grad_f = grad_mixed.astype(jnp.float32)
    scores = jnp.einsum('amc,bmc->mab', query_f, key_f) * scale
    top = lax.optimization_barrier(jnp.max(scores, axis=-1, keepdims=True))
    expo = jnp.exp(scores - top)
    prob_f = expo / lax.optimization_barrier(jnp.sum(expo, axis=-1, keepdims=True))
    prob = rounded(prob_f).astype(jnp.float32)
    mixed = rounded(jnp.einsum('mab,bmc->amc', prob, value_f))
    grad_prob = jnp.einsum('amc,bmc->mab', grad_f, value_f)
    grad_value = rounded(jnp.einsum('mab,amc->bmc', prob, grad_f))
    inner = lax.optimization_barrier(jnp.sum(prob_f * grad_prob, axis=-1, keepdims=True))
    grad_score = rounded(prob_f * (grad_prob - inner) * scale).astype(jnp.float32)
    grad_query = rounded(jnp.einsum('mab,bmc->amc', grad_score, key_f))
    grad_key = rounded(jnp.einsum('mab,amc->bmc', grad_score, query_f))
    return (mixed, grad_query, grad_key, grad_value)

def project(flat, weight):
    return rounded(jnp.dot(flat.astype(jnp.float32), weight.astype(jnp.float32)))

def reference(features, cotangent, conv_first, conv_second, w_query, w_key, w_value, w_out):
    views = features.shape[0]
    chan = features.shape[3]
    inputs_f = features.astype(jnp.float32)
    act_first = rounded(jax.nn.silu(inputs_f))
    pad_first = pad_cells(act_first)
    hidden_first = rounded(convolve(pad_first, conv_first))
    act_second = rounded(jax.nn.silu(hidden_first.astype(jnp.float32)))
    pad_second = pad_cells(act_second)
    summed = rounded(inputs_f + convolve(pad_second, conv_second))
    summed_f = summed.astype(jnp.float32)
    centred = summed_f - lax.optimization_barrier(jnp.mean(summed_f, axis=-1, keepdims=True))
    inv_scale = lax.rsqrt(lax.optimization_barrier(jnp.mean(centred * centred, axis=-1, keepdims=True)) + 1e-05)
    normed_f = centred * inv_scale
    normed = rounded(normed_f)
    flat_normed = normed.reshape(-1, chan)
    flat_cot = cotangent.reshape(-1, chan)
    query = project(flat_normed, w_query)
    key = project(flat_normed, w_key)
    value = project(flat_normed, w_value)
    grad_mixed = project(flat_cot, jnp.transpose(w_out))
    shaped = lambda array: array.reshape(views, -1, chan)
    mixed, grad_query, grad_key, grad_value = attend(shaped(query), shaped(key), shaped(value), shaped(grad_mixed))
    mixed = mixed.reshape(-1, chan).astype(jnp.float32)
    grad_query = grad_query.reshape(-1, chan).astype(jnp.float32)
    grad_key = grad_key.reshape(-1, chan).astype(jnp.float32)
    grad_value = grad_value.reshape(-1, chan).astype(jnp.float32)
    normed_ff = flat_normed.astype(jnp.float32)
    contract = (((0,), (0,)), ((), ()))
    attn_grads = jnp.stack([lax.dot_general(normed_ff, grad_query, contract), lax.dot_general(normed_ff, grad_key, contract), lax.dot_general(normed_ff, grad_value, contract), lax.dot_general(mixed, flat_cot.astype(jnp.float32), contract)])
    back = jnp.dot(grad_query, jnp.transpose(w_query).astype(jnp.float32))
    back = back + jnp.dot(grad_key, jnp.transpose(w_key).astype(jnp.float32))
    back = back + jnp.dot(grad_value, jnp.transpose(w_value).astype(jnp.float32))
    grad_normed = rounded(back).astype(jnp.float32).reshape(features.shape)
    grad_summed = cotangent.astype(jnp.float32) + inv_scale * (grad_normed - lax.optimization_barrier(jnp.mean(grad_normed, axis=-1, keepdims=True)) - normed_f * lax.optimization_barrier(jnp.mean(grad_normed * normed_f, axis=-1, keepdims=True)))
    grad_second = rounded(grad_summed)
    slope_second = convolve(pad_cells(grad_second), flipped(conv_second))
    grad_first = rounded(slope_second * silu_slope(hidden_first.astype(jnp.float32)))
    slope_first = convolve(pad_cells(grad_first), flipped(conv_first))
    grad_features = (grad_summed + slope_first * silu_slope(inputs_f)).astype(jnp.bfloat16)
    conv_grads = jnp.stack([kernel_grad(pad_first, grad_first), kernel_grad(pad_second, grad_second)])
    return (grad_features, conv_grads, attn_grads)
```

```python
import functools

import jax
import jax.numpy as jnp
from jax import lax
from jax.experimental import pallas as pl
from jax.experimental.pallas import tpu as pltpu
from jax.sharding import PartitionSpec as P

MESH = pl.DeviceIdType.MESH
F32 = jnp.float32
BF16 = jnp.bfloat16
NT = (((1,), (1,)), ((), ()))
TN = (((0,), (0,)), ((), ()))
CHUNKS = 2
DEEP = 2


def dot(a, b):
    return jnp.dot(a, b, preferred_element_type=F32)


def dot_nt(a, b):
    return lax.dot_general(a, b, NT, preferred_element_type=F32)


def dot_tn(a, b):
    return lax.dot_general(a, b, TN, preferred_element_type=F32)


def silu(x):
    return x * jax.nn.sigmoid(x)


def silu_slope(x):
    sigma = jax.nn.sigmoid(x)
    return sigma * (1.0 + x * (1.0 - sigma))


def mark(name):
    pass


def kernel(dims, names, *refs):
    run(dims, **dict(zip(names, refs, strict=True)))


def run(
    dims, feat, cot, w1h, w2h, wqh, wkh, wvh, woh, gfeat, conv_out, attn_out,
    w1, w2, wq, wk, wv, wo, load,
    fmap, cotv, cols1, cols2, colsg, hidden, normed, normed_f, inv, g2, gs, g1,
    normp, cotp, backp, gn, gq, gk, gv, mx,
    part_a, part_b, part_c, r1a, r1b, r1c, t1a, t1b, t1c, r2a, r2b, r2c,
    t2a, t2b, t2c, r3a, r3b, r3c, r4a, r4b, r4c,
    halo_send, halo_recv, cot_send, cot_recv, nrm_send, nrm_recv, bck_send, bck_recv,
    s1_send, s1_recv, s2_send, s2_recv, s3_send, s3_recv, s4_send, s4_recv,
):
    views, strips, rows, width, chan = dims
    pixels = rows * width
    half = pixels // CHUNKS
    share = half // views
    edge = DEEP * width
    zs = views // 2
    view = lax.axis_index("view")
    strip = lax.axis_index("strip")
    core = lax.rem(view, 2)
    zed = lax.div(view, 2)

    barrier = pltpu.get_barrier_semaphore()
    for k in range(1, views):
        pl.semaphore_signal(
            barrier, inc=1, device_id={"view": lax.rem(view + k, views)}, device_id_type=MESH
        )
    for k in range(1, strips):
        pl.semaphore_signal(
            barrier, inc=1, device_id={"strip": lax.rem(strip + k, strips)}, device_id_type=MESH
        )
    mine = pl.ds(pl.multiple_of(view * share, share), share)
    loads = [
        pltpu.make_async_copy(src, dst, load.at[i])
        for i, (src, dst) in enumerate(
            (
                (feat, fmap.at[pl.ds(edge, pixels)]),
                (w1h, w1), (w2h, w2), (woh, wo), (wqh, wq), (wkh, wk), (wvh, wv),
                (cot.at[:, mine], cotp.at[:, mine]), (cot, cotv),
            )
        )
    ]
    for item in loads:
        item.start()

    @pl.when(strip == 0)
    def _():
        fmap[pl.ds(0, edge)] = jnp.zeros((edge, chan), BF16)
        g2[pl.ds(0, edge)] = jnp.zeros((edge, chan), BF16)

    @pl.when(strip == strips - 1)
    def _():
        fmap[pl.ds(edge + pixels, edge)] = jnp.zeros((edge, chan), BF16)
        g2[pl.ds(edge + pixels, edge)] = jnp.zeros((edge, chan), BF16)

    pl.semaphore_wait(barrier, views - 1 + strips - 1)

    def halo_copy(e, src, dst, way):
        start = 0 if way == 0 else pixels - edge
        land = edge + pixels if way == 0 else 0
        near = lax.max(strip - 1, 0) if way == 0 else lax.min(strip + 1, strips - 1)
        base = edge if src is dst else 0
        return pltpu.make_async_remote_copy(
            src_ref=src.at[pl.ds(base + start, edge)], dst_ref=dst.at[pl.ds(land, edge)],
            send_sem=halo_send.at[e, way], recv_sem=halo_recv.at[e, way],
            device_id={"strip": near}, device_id_type=MESH,
        )

    def halo_start(e, src, dst, way):
        copy = halo_copy(e, src, dst, way)
        pl.when(strip > 0 if way == 0 else strip < strips - 1)(copy.start)

    def halo_sent(e, src, dst, way):
        copy = halo_copy(e, src, dst, way)
        pl.when(strip > 0 if way == 0 else strip < strips - 1)(copy.wait_send)

    def halo_here(e, src, dst, way):
        copy = halo_copy(e, src, dst, way)
        pl.when(strip < strips - 1 if way == 0 else strip > 0)(copy.wait_recv)

    def spread(src, dst, send, recv):
        out = []
        for k in range(1, views):
            peer = lax.rem(view + k, views)
            out.append(
                pltpu.make_async_remote_copy(
                    src_ref=src(pl.ds(pl.multiple_of(peer * share, share), share)),
                    dst_ref=dst(mine),
                    send_sem=send(k), recv_sem=recv(k),
                    device_id={"view": peer}, device_id_type=MESH,
                )
            )
        return out

    def start(copies):
        for copy in copies:
            copy.start()

    def wait(copies):
        for copy in copies:
            copy.wait()

    def build(cols, offset, x):
        count = x.shape[0]
        column = lax.rem(lax.broadcasted_iota(jnp.int32, (count, chan), 0), width)
        left = jnp.where(column == 0, 0.0, pltpu.roll(x, 1, 0))
        right = jnp.where(column == width - 1, 0.0, pltpu.roll(x, count - 1, 0))
        cols[pl.ds(offset, count), pl.ds(0, chan)] = left.astype(BF16)
        cols[pl.ds(offset, count), pl.ds(chan, chan)] = x.astype(BF16)
        cols[pl.ds(offset, count), pl.ds(2 * chan, chan)] = right.astype(BF16)

    def conv(cols, w, offset, count):
        total = None
        for r in range(3):
            term = dot(cols[pl.ds(offset + r * width, count), :], w[r])
            total = term if total is None else total + term
        return total

    def conv_flip(cols, w, offset, count):
        total = None
        for r in range(3):
            for s in range(3):
                term = dot_nt(
                    cols[pl.ds(offset + r * width, count), pl.ds(s * chan, chan)],
                    w[2 - r, pl.ds((2 - s) * chan, chan), :],
                )
                total = term if total is None else total + term
        return total

    def wgrad(cols, offset, d, out):
        pieces, _, _, parts, unit, _ = out.shape
        per = 3 * chan // unit
        for r in range(3):
            value = dot_tn(cols[pl.ds(offset + r * width, pixels), :], d).astype(BF16)
            for m in range(per):
                u = r * per + m
                v, rest = divmod(u, pieces * parts)
                p, t = divmod(rest, parts)
                out[p, v // 2, v % 2, t] = value[m * unit : (m + 1) * unit]

    def inside(x, first, last):
        if first:
            low = lax.broadcasted_iota(jnp.int32, x.shape, 0)
            x = jnp.where(jnp.logical_and(low < width, strip == 0), 0.0, x)
        if last:
            high = lax.broadcasted_iota(jnp.int32, x.shape, 0)
            gone = jnp.logical_and(high >= x.shape[0] - width, strip == strips - 1)
            x = jnp.where(gone, 0.0, x)
        return x

    def group(base, part, r1, t1, r2, t2, r3, r4):
        parts = part.shape[3]

        def stage1(p):
            return [
                pltpu.make_async_remote_copy(
                    src_ref=part.at[p, :, 1 - core], dst_ref=r1.at[p],
                    send_sem=s1_send.at[base + p], recv_sem=s1_recv.at[base + p],
                    device_id={"view": view + 1 - 2 * core}, device_id_type=MESH,
                )
            ]

        def reduce1(p):
            for j in range(zs):
                for t in range(parts):
                    t1[p, t, j] = (
                        part[p, j, core, t].astype(F32) + r1[p, j, t].astype(F32)
                    ).astype(BF16)

        def stage2(p):
            out = []
            for k in range(1, parts):
                other = lax.rem(strip + k, strips)
                out.append(
                    pltpu.make_async_remote_copy(
                        src_ref=t1.at[p, other], dst_ref=r2.at[p, k - 1],
                        send_sem=s2_send.at[base + p, k], recv_sem=s2_recv.at[base + p, k],
                        device_id={"strip": other}, device_id_type=MESH,
                    )
                )
            return out

        def reduce2(p):
            own = strip if parts > 1 else 0
            for j in range(zs):
                value = t1[p, own, j].astype(F32)
                for k in range(1, parts):
                    value = value + r2[p, k - 1, j].astype(F32)
                t2[p, j] = value.astype(BF16)

        def stage3(p):
            out = []
            for k in range(1, zs):
                other = lax.rem(zed + k, zs)
                out.append(
                    pltpu.make_async_remote_copy(
                        src_ref=t2.at[p, other], dst_ref=r3.at[p, k - 1],
                        send_sem=s3_send.at[base + p, k], recv_sem=s3_recv.at[base + p, k],
                        device_id={"view": other * 2 + core}, device_id_type=MESH,
                    )
                )
            return out

        def reduce3(p):
            value = t2[p, zed].astype(F32)
            for k in range(1, zs):
                value = value + r3[p, k - 1].astype(F32)
            r4[p, strip] = value.astype(BF16)

        def stage4(p):
            out = []
            for k in range(1, strips):
                out.append(
                    pltpu.make_async_remote_copy(
                        src_ref=r4.at[p, strip], dst_ref=r4.at[p, strip],
                        send_sem=s4_send.at[base + p, k], recv_sem=s4_recv.at[base + p, k],
                        device_id={"strip": lax.rem(strip + k, strips)}, device_id_type=MESH,
                    )
                )
            return out

        def final(p):
            if parts > 1:
                return [r4[p, t].astype(F32) for t in range(parts)]
            value = r4[p, 0].astype(F32)
            for t in range(1, strips):
                value = value + r4[p, t].astype(F32)
            return [value]

        reduces = (None, reduce1, reduce2, reduce3)
        stages = (stage1, stage2, stage3, stage4)

        def launch():
            for p in range(part.shape[0]):
                start(stage1(p))

        def advance(k, p):
            wait(stages[k - 1](p))
            reduces[k](p)
            start(stages[k](p))

        def advance_all(k):
            for p in range(part.shape[0]):
                advance(k, p)

        def finish(store):
            for p in range(part.shape[0]):
                wait(stage4(p))
                for t, value in enumerate(final(p)):
                    store(p * parts + t, value)

        return launch, advance_all, finish

    count_a = part_a.shape[0]
    count_b = part_b.shape[0]
    launch_a, step_a, finish_a = group(0, part_a, r1a, t1a, r2a, t2a, r3a, r4a)
    launch_b, step_b, finish_b = group(count_a, part_b, r1b, t1b, r2b, t2b, r3b, r4b)
    launch_c, step_c, finish_c = group(count_a + count_b, part_c, r1c, t1c, r2c, t2c, r3c, r4c)

    halo_start(0, feat, fmap, 0)
    halo_start(0, feat, fmap, 1)
    cot_copies = spread(
        lambda s: cot.at[:, s], lambda s: cotp.at[:, s],
        lambda k: cot_send.at[k], lambda k: cot_recv.at[k],
    )
    start(cot_copies)

    def forward(row, count, first=False, last=False):
        out = conv(cols1, w1, row * width, count * width).astype(BF16)
        hidden[pl.ds(row * width, count * width)] = out
        act = silu(out.astype(F32)).astype(BF16).astype(F32)
        build(cols2, row * width, inside(act, first, last))

    def nrm_copies(h):
        return spread(
            lambda s: normed.at[h, s], lambda s: normp.at[h, s],
            lambda k: nrm_send.at[h, k], lambda k: nrm_recv.at[h, k],
        )

    def norm(h):
        offset = h * half
        x = fmap[pl.ds(edge + offset, half)].astype(F32)
        summed = (x + conv(cols2, w2, offset, half)).astype(BF16).astype(F32)
        centred = summed - jnp.mean(summed, axis=-1, keepdims=True)
        scale = lax.rsqrt(jnp.mean(centred * centred, axis=-1, keepdims=True) + 1e-05)
        inv[h] = jnp.broadcast_to(scale, (half, 128))
        nf = centred * scale
        normed_f[h] = nf
        normed[h] = nf.astype(BF16)
        start(nrm_copies(h))
        normp[h, mine] = normed[h, mine]

    loads[0].wait()
    build(cols1, edge, silu(fmap[pl.ds(edge, pixels)].astype(F32)))
    loads[1].wait()
    forward(DEEP, rows - DEEP)
    halo_here(0, feat, fmap, 1)
    build(cols1, 0, silu(fmap[pl.ds(0, edge)].astype(F32)))
    forward(0, DEEP, first=True)
    loads[2].wait()
    norm(0)
    halo_here(0, feat, fmap, 0)
    build(cols1, edge + pixels, silu(fmap[pl.ds(edge + pixels, edge)].astype(F32)))
    forward(rows, DEEP, last=True)
    norm(1)
    mark("normed")

    for item in loads[3:]:
        item.wait()
    wait(cot_copies)
    gmix = dot_nt(cotp[...].reshape(pixels, chan), wo[...]).astype(BF16)
    ia = lax.rem(lax.broadcasted_iota(jnp.int32, (half, half), 0), share)
    ib = lax.rem(lax.broadcasted_iota(jnp.int32, (half, half), 1), share)
    same = ia == ib
    factor = chan ** (-0.5)

    def bck_copies(h):
        return spread(
            lambda s: backp.at[h, s], lambda s: gn.at[h, s],
            lambda k: bck_send.at[h, k], lambda k: bck_recv.at[h, k],
        )

    def attend(h):
        rp = normp[h]
        gm = gmix[h * half : (h + 1) * half]
        query = dot(rp, wq[...]).astype(BF16)
        key = dot(rp, wk[...]).astype(BF16)
        value = dot(rp, wv[...]).astype(BF16)
        scores = jnp.where(same, dot_nt(query, key) * factor, -jnp.inf)
        expo = jnp.exp(scores - jnp.max(scores, axis=-1, keepdims=True))
        prob_f = expo / jnp.sum(expo, axis=-1, keepdims=True)
        prob = prob_f.astype(BF16)
        grad_prob = dot_nt(gm, value)
        inner = jnp.sum(prob_f * grad_prob, axis=-1, keepdims=True)
        grad_score = (prob_f * (grad_prob - inner) * factor).astype(BF16)
        grad_value = dot_tn(prob, gm).astype(BF16)
        grad_query = dot(grad_score, key).astype(BF16)
        grad_key = dot_tn(grad_score, query).astype(BF16)
        back = (
            dot_nt(grad_query, wq[...]) + dot_nt(grad_key, wk[...]) + dot_nt(grad_value, wv[...])
        )
        backp[h] = back.astype(BF16)
        start(bck_copies(h))
        gn[h, mine] = backp[h, mine]
        gq[h] = grad_query
        gk[h] = grad_key
        gv[h] = grad_value
        mx[h] = dot(prob, value).astype(BF16)

    for h in range(CHUNKS):
        wait(nrm_copies(h))
        attend(h)
    mark("attended")
    parts = part_a.shape[3]
    unit = chan // (views * parts)
    for t, (lhs, rhs) in enumerate(((normp, gq), (normp, gk), (normp, gv), (mx, cotp))):
        term = dot_tn(
            lhs[...].reshape(pixels, chan), rhs[...].reshape(pixels, chan)
        ).astype(BF16)
        for u in range(views * parts):
            v, q = divmod(u, parts)
            part_a[0, v // 2, v % 2, q, t] = term[u * unit : (u + 1) * unit]
    launch_a()

    def backward(h):
        gnf = gn[h].astype(F32)
        nf = normed_f[h]
        gsum = cotv[h].astype(F32) + inv[h, :, 0:1] * (
            gnf
            - jnp.mean(gnf, axis=-1, keepdims=True)
            - nf * jnp.mean(gnf * nf, axis=-1, keepdims=True)
        )
        gs[h] = gsum
        g2[pl.ds(edge + h * half, half)] = gsum.astype(BF16)

    step_a(1)
    for h in range(CHUNKS):
        wait(bck_copies(h))
        backward(h)
        if h == 0:
            halo_start(1, g2, g2, 0)
    halo_start(1, g2, g2, 1)
    mark("g2")
    wgrad(cols2, 0, g2[pl.ds(edge, pixels)], part_b)
    launch_b()
    build(colsg, edge, g2[pl.ds(edge, pixels)].astype(F32))
    step_a(2)
    step_b(1)

    def flipped(row, count, first=False, last=False):
        slope = conv_flip(colsg, w2, row * width, count * width)
        own = slope * silu_slope(hidden[pl.ds(row * width, count * width)].astype(F32))
        g1[pl.ds(row * width, count * width)] = inside(own, first, last).astype(BF16)

    halo_here(1, g2, g2, 1)
    build(colsg, 0, g2[pl.ds(0, edge)].astype(F32))
    halo_here(1, g2, g2, 0)
    build(colsg, edge + pixels, g2[pl.ds(edge + pixels, edge)].astype(F32))
    flipped(0, rows + 2, True, True)
    mark("g1")
    wgrad(cols1, width, g1[pl.ds(width, pixels)], part_c)
    launch_c()
    build(colsg, 0, g1[...].astype(F32))
    step_c(1)
    step_b(2)
    slope = conv_flip(colsg, w1, 0, pixels)
    gfeat[...] = (
        gs[...].reshape(pixels, chan)
        + slope * silu_slope(fmap[pl.ds(edge, pixels)].astype(F32))
    ).astype(BF16)
    step_a(3)
    step_c(2)
    step_b(3)
    step_c(3)

    for way in range(2):
        halo_sent(0, feat, fmap, way)
        halo_sent(1, g2, g2, way)

    def store_a(u, value):
        attn_out[:, pl.ds(u * unit, unit), :] = value.astype(attn_out.dtype)

    def store_conv(i):
        def store(u, value):
            size = value.shape[0]
            conv_out[i, pl.ds(u * size, size), :] = value.astype(conv_out.dtype)

        return store

    finish_a(store_a)
    finish_b(store_conv(1))
    finish_c(store_conv(0))


def widen(a, b, c, x, y, z):
    x[...] = a[...]
    y[...] = b[...].astype(F32)
    z[...] = c[...].astype(F32)


def body(features, cotangent, conv_first, conv_second, w_query, w_key, w_value, w_out):
    views = lax.axis_size("view")
    strips = lax.axis_size("strip")
    _, rows, width, chan = features.shape
    pixels = rows * width
    zs = views // 2
    cut = 9 * chan // views
    slab = chan // views
    vm = pltpu.VMEM
    dma = pltpu.SemaphoreType.DMA
    flat = (pixels, chan)
    split = (CHUNKS, pixels // CHUNKS, chan)
    wide = (rows + 2 * DEEP) * width
    near = (rows + 2) * width
    exact = cut % (16 * strips) == 0 and slab % (16 * strips) == 0
    parts = strips if exact else 1
    pieces = 3 if cut % (48 * parts) == 0 else 1
    conv_u = (cut // (parts * pieces), chan)
    attn_u = (4, slab // parts, chan)
    units = ((1, attn_u), (pieces, conv_u), (pieces, conv_u))
    total = 1 + 2 * pieces
    hold = {
        "part_": [(n, zs, 2, parts) + u for n, u in units],
        "r1": [(n, zs, parts) + u for n, u in units],
        "t1": [(n, parts, zs) + u for n, u in units],
        "r2": [(n, max(parts - 1, 1), zs) + u for n, u in units],
        "t2": [(n, zs) + u for n, u in units],
        "r3": [(n, zs - 1) + u for n, u in units],
        "r4": [(n, strips) + u for n, u in units],
    }
    conv_k = (3, 3 * chan, chan)
    square = (chan, chan)
    scratch = {
        "w1": vm(conv_k, BF16), "w2": vm(conv_k, BF16),
        "wq": vm(square, BF16), "wk": vm(square, BF16),
        "wv": vm(square, BF16), "wo": vm(square, BF16), "load": dma((9,)),
        "fmap": vm((wide, chan), BF16), "cotv": vm(split, BF16),
        "cols1": vm((wide, 3 * chan), BF16), "cols2": vm((near, 3 * chan), BF16),
        "colsg": vm((wide, 3 * chan), BF16),
        "hidden": vm((near, chan), BF16), "normed": vm(split, BF16), "normed_f": vm(split, F32),
        "inv": vm(split[:2] + (128,), F32), "g2": vm((wide, chan), BF16), "gs": vm(split, F32),
        "g1": vm((near, chan), BF16),
    }
    for name in ("normp", "cotp", "backp", "gn", "gq", "gk", "gv", "mx"):
        scratch[name] = vm(split, BF16)
    for name, shapes in hold.items():
        for letter, shape in zip("abc", shapes):
            scratch[name + letter] = vm(shape, BF16)
    counts = {
        "halo": (2, 2), "cot": (views,), "nrm": (CHUNKS, views), "bck": (CHUNKS, views),
        "s1": (total,), "s2": (total, strips), "s3": (total, zs), "s4": (total, strips),
    }
    for name, shape in counts.items():
        scratch[name + "_send"] = dma(shape)
        scratch[name + "_recv"] = dma(shape)
    names = (
        "feat", "cot", "w1h", "w2h", "wqh", "wkh", "wvh", "woh", "gfeat", "conv_out", "attn_out",
    ) + tuple(scratch)
    spec = pl.BlockSpec(memory_space=pltpu.VMEM)
    stay = pl.BlockSpec(memory_space=pl.ANY)
    kind = BF16 if exact else F32
    conv_s = (2, cut, chan)
    attn_s = (4, slab, chan)
    outs = pl.pallas_call(
        functools.partial(kernel, (views, strips, rows, width, chan), names),
        out_shape=(
            jax.ShapeDtypeStruct(flat, BF16),
            jax.ShapeDtypeStruct(conv_s, kind),
            jax.ShapeDtypeStruct(attn_s, kind),
        ),
        in_specs=[stay] * 8,
        out_specs=(spec, spec, spec),
        scratch_shapes=list(scratch.values()),
        compiler_params=pltpu.CompilerParams(
            collective_id=0, has_side_effects=True, vmem_limit_bytes=56 * 1024 * 1024
        ),
    )(
        features.reshape(flat),
        cotangent.reshape(split),
        conv_first.reshape(3, 3 * chan, chan),
        conv_second.reshape(3, 3 * chan, chan),
        w_query, w_key, w_value, w_out,
    )
    outs = pl.pallas_call(
        widen,
        out_shape=(
            jax.ShapeDtypeStruct(flat, BF16),
            jax.ShapeDtypeStruct(conv_s, F32),
            jax.ShapeDtypeStruct(attn_s, F32),
        ),
        in_specs=[spec] * 3,
        out_specs=(spec, spec, spec),
    )(*outs)
    return (outs[0].reshape(features.shape), outs[1], outs[2])


def solution(mesh):
    rows = P(("orbit", "view"), "strip", None, None)
    grads = P("orbit", "view", None)
    return jax.shard_map(
        body,
        mesh=mesh,
        in_specs=(rows, rows, P(), P(), P(), P(), P(), P()),
        out_specs=(rows, grads, grads),
        check_vma=False,
    )
```

```python
import functools

import jax
import jax.numpy as jnp
from jax import lax
from jax.experimental import pallas as pl
from jax.experimental.pallas import tpu as pltpu
from jax.sharding import PartitionSpec as P

MESH = pl.DeviceIdType.MESH
F32 = jnp.float32
BF16 = jnp.bfloat16
NT = (((1,), (1,)), ((), ()))
TN = (((0,), (0,)), ((), ()))
CHUNKS = 2
DEEP = 2


def dot(a, b):
    return jnp.dot(a, b, preferred_element_type=F32)


def dot_nt(a, b):
    return lax.dot_general(a, b, NT, preferred_element_type=F32)


def dot_tn(a, b):
    return lax.dot_general(a, b, TN, preferred_element_type=F32)


def silu(x):
    return x * jax.nn.sigmoid(x)


def silu_slope(x):
    sigma = jax.nn.sigmoid(x)
    return sigma * (1.0 + x * (1.0 - sigma))


def group(place, sems, start, wait, base, part, r1, t1, r2, t2, r3, r4):
    view, strip, core, zed, views, strips, zs = place
    s1_send, s1_recv, s2_send, s2_recv, s3_send, s3_recv, s4_send, s4_recv = sems
    parts = part.shape[3]
    shares = t1 is None or parts > 1

    def stage1(p):
        return [
            pltpu.make_async_remote_copy(
                src_ref=part.at[p, :, 1 - core], dst_ref=r1.at[p],
                send_sem=s1_send.at[base + p], recv_sem=s1_recv.at[base + p],
                device_id={"view": view + 1 - 2 * core}, device_id_type=MESH,
            )
        ]

    def reduce1(p):
        for j in range(zs):
            if t1 is None:
                t2[p, j] = (
                    part[p, j, core, 0].astype(F32) + r1[p, j, 0].astype(F32)
                ).astype(BF16)
                continue
            for t in range(parts):
                t1[p, t, j] = (
                    part[p, j, core, t].astype(F32) + r1[p, j, t].astype(F32)
                ).astype(BF16)

    def stage2(p):
        out = []
        for k in range(1, parts):
            other = lax.rem(strip + k, strips)
            out.append(
                pltpu.make_async_remote_copy(
                    src_ref=t1.at[p, other], dst_ref=r2.at[p, k - 1],
                    send_sem=s2_send.at[base + p, k], recv_sem=s2_recv.at[base + p, k],
                    device_id={"strip": other}, device_id_type=MESH,
                )
            )
        return out

    def reduce2(p):
        own = strip if parts > 1 else 0
        for j in range(zs):
            value = t1[p, own, j].astype(F32)
            for k in range(1, parts):
                value = value + r2[p, k - 1, j].astype(F32)
            t2[p, j] = value.astype(BF16)

    def stage3(p):
        out = []
        for k in range(1, zs):
            other = lax.rem(zed + k, zs)
            out.append(
                pltpu.make_async_remote_copy(
                    src_ref=t2.at[p, other], dst_ref=r3.at[p, k - 1],
                    send_sem=s3_send.at[base + p, k], recv_sem=s3_recv.at[base + p, k],
                    device_id={"view": other * 2 + core}, device_id_type=MESH,
                )
            )
        return out

    def reduce3(p):
        value = t2[p, zed].astype(F32)
        for k in range(1, zs):
            value = value + r3[p, k - 1].astype(F32)
        r4[p, strip] = value.astype(BF16)

    def stage4(p):
        out = []
        for k in range(1, strips):
            out.append(
                pltpu.make_async_remote_copy(
                    src_ref=r4.at[p, strip], dst_ref=r4.at[p, strip],
                    send_sem=s4_send.at[base + p, k], recv_sem=s4_recv.at[base + p, k],
                    device_id={"strip": lax.rem(strip + k, strips)}, device_id_type=MESH,
                )
            )
        return out

    def final(p):
        if shares:
            return [r4[p, t].astype(F32) for t in range(strips)]
        value = r4[p, 0].astype(F32)
        for t in range(1, strips):
            value = value + r4[p, t].astype(F32)
        return [value]

    reduces = (None, reduce1, reduce2, reduce3)
    stages = (stage1, stage2, stage3, stage4)
    if t1 is None:
        reduces = (None, reduce1, reduce3)
        stages = (stage1, stage3, stage4)

    def launch():
        for p in range(part.shape[0]):
            start(stage1(p))

    def advance(k, p):
        wait(stages[k - 1](p))
        reduces[k](p)
        start(stages[k](p))

    def advance_all(k):
        for p in range(part.shape[0]):
            advance(k, p)

    def finish(store):
        for p in range(part.shape[0]):
            wait(stage4(p))
            for t, value in enumerate(final(p)):
                store(p * (strips if shares else 1) + t, value)

    return launch, advance_all, finish


def mark(name):
    pass


def kernel(call, dims, names, *refs):
    call(dims, **dict(zip(names, refs, strict=True)))


def run(
    dims, feat, cot, w1h, w2h, wqh, wkh, wvh, woh, gfeat, conv_out, attn_out,
    w1, w2, wq, wk, wv, wo, load,
    fmap, cotv, cols1, cols2, colsg, hidden, normed, normed_f, inv, g2, gs, g1,
    normp, cotp, backp, gn, gq, gk, gv, mx,
    part_a, part_b, part_c, r1a, r1b, r1c, t1a, t1b, t1c, r2a, r2b, r2c,
    t2a, t2b, t2c, r3a, r3b, r3c, r4a, r4b, r4c,
    halo_send, halo_recv, cot_send, cot_recv, nrm_send, nrm_recv, bck_send, bck_recv,
    s1_send, s1_recv, s2_send, s2_recv, s3_send, s3_recv, s4_send, s4_recv,
):
    views, strips, rows, width, chan = dims
    pixels = rows * width
    half = pixels // CHUNKS
    share = half // views
    edge = DEEP * width
    zs = views // 2
    view = lax.axis_index("view")
    strip = lax.axis_index("strip")
    core = lax.rem(view, 2)
    zed = lax.div(view, 2)

    barrier = pltpu.get_barrier_semaphore()
    for k in range(1, views):
        pl.semaphore_signal(
            barrier, inc=1, device_id={"view": lax.rem(view + k, views)}, device_id_type=MESH
        )
    for k in range(1, strips):
        pl.semaphore_signal(
            barrier, inc=1, device_id={"strip": lax.rem(strip + k, strips)}, device_id_type=MESH
        )
    mine = pl.ds(pl.multiple_of(view * share, share), share)
    loads = [
        pltpu.make_async_copy(src, dst, load.at[i])
        for i, (src, dst) in enumerate(
            (
                (feat, fmap.at[pl.ds(edge, pixels)]),
                (w1h, w1), (w2h, w2), (woh, wo), (wqh, wq), (wkh, wk), (wvh, wv),
                (cot.at[:, mine], cotp.at[:, mine]), (cot, cotv),
            )
        )
    ]
    for item in loads:
        item.start()

    @pl.when(strip == 0)
    def _():
        fmap[pl.ds(0, edge)] = jnp.zeros((edge, chan), BF16)
        g2[pl.ds(0, edge)] = jnp.zeros((edge, chan), BF16)

    @pl.when(strip == strips - 1)
    def _():
        fmap[pl.ds(edge + pixels, edge)] = jnp.zeros((edge, chan), BF16)
        g2[pl.ds(edge + pixels, edge)] = jnp.zeros((edge, chan), BF16)

    pl.semaphore_wait(barrier, views - 1 + strips - 1)

    def halo_copy(e, src, dst, way):
        start = 0 if way == 0 else pixels - edge
        land = edge + pixels if way == 0 else 0
        near = lax.max(strip - 1, 0) if way == 0 else lax.min(strip + 1, strips - 1)
        base = edge if src is dst else 0
        return pltpu.make_async_remote_copy(
            src_ref=src.at[pl.ds(base + start, edge)], dst_ref=dst.at[pl.ds(land, edge)],
            send_sem=halo_send.at[e, way], recv_sem=halo_recv.at[e, way],
            device_id={"strip": near}, device_id_type=MESH,
        )

    def halo_start(e, src, dst, way):
        copy = halo_copy(e, src, dst, way)
        pl.when(strip > 0 if way == 0 else strip < strips - 1)(copy.start)

    def halo_sent(e, src, dst, way):
        copy = halo_copy(e, src, dst, way)
        pl.when(strip > 0 if way == 0 else strip < strips - 1)(copy.wait_send)

    def halo_here(e, src, dst, way):
        copy = halo_copy(e, src, dst, way)
        pl.when(strip < strips - 1 if way == 0 else strip > 0)(copy.wait_recv)

    def spread(src, dst, send, recv):
        out = []
        for k in range(1, views):
            peer = lax.rem(view + k, views)
            out.append(
                pltpu.make_async_remote_copy(
                    src_ref=src(pl.ds(pl.multiple_of(peer * share, share), share)),
                    dst_ref=dst(mine),
                    send_sem=send(k), recv_sem=recv(k),
                    device_id={"view": peer}, device_id_type=MESH,
                )
            )
        return out

    def start(copies):
        for copy in copies:
            copy.start()

    def wait(copies):
        for copy in copies:
            copy.wait()

    def build(cols, offset, x):
        count = x.shape[0]
        column = lax.rem(lax.broadcasted_iota(jnp.int32, (count, chan), 0), width)
        left = jnp.where(column == 0, 0.0, pltpu.roll(x, 1, 0))
        right = jnp.where(column == width - 1, 0.0, pltpu.roll(x, count - 1, 0))
        cols[pl.ds(offset, count), pl.ds(0, chan)] = left.astype(BF16)
        cols[pl.ds(offset, count), pl.ds(chan, chan)] = x.astype(BF16)
        cols[pl.ds(offset, count), pl.ds(2 * chan, chan)] = right.astype(BF16)

    def conv(cols, w, offset, count):
        total = None
        for r in range(3):
            term = dot(cols[pl.ds(offset + r * width, count), :], w[r])
            total = term if total is None else total + term
        return total

    def conv_flip(cols, w, offset, count):
        total = None
        for r in range(3):
            for s in range(3):
                term = dot_nt(
                    cols[pl.ds(offset + r * width, count), pl.ds(s * chan, chan)],
                    w[2 - r, pl.ds((2 - s) * chan, chan), :],
                )
                total = term if total is None else total + term
        return total

    def wgrad(cols, offset, d, out):
        pieces, _, _, parts, unit, _ = out.shape
        per = 3 * chan // unit
        for r in range(3):
            value = dot_tn(cols[pl.ds(offset + r * width, pixels), :], d).astype(BF16)
            for m in range(per):
                u = r * per + m
                v, rest = divmod(u, pieces * parts)
                p, t = divmod(rest, parts)
                out[p, v // 2, v % 2, t] = value[m * unit : (m + 1) * unit]

    def inside(x, first, last):
        if first:
            low = lax.broadcasted_iota(jnp.int32, x.shape, 0)
            x = jnp.where(jnp.logical_and(low < width, strip == 0), 0.0, x)
        if last:
            high = lax.broadcasted_iota(jnp.int32, x.shape, 0)
            gone = jnp.logical_and(high >= x.shape[0] - width, strip == strips - 1)
            x = jnp.where(gone, 0.0, x)
        return x

    sems = (s1_send, s1_recv, s2_send, s2_recv, s3_send, s3_recv, s4_send, s4_recv)
    place = (view, strip, core, zed, views, strips, zs)
    count_a = part_a.shape[0]
    count_b = part_b.shape[0]
    launch_a, step_a, finish_a = group(
        place, sems, start, wait, 0, part_a, r1a, t1a, r2a, t2a, r3a, r4a
    )
    launch_b, step_b, finish_b = group(
        place, sems, start, wait, count_a, part_b, r1b, t1b, r2b, t2b, r3b, r4b
    )
    launch_c, step_c, finish_c = group(
        place, sems, start, wait, count_a + count_b, part_c, r1c, t1c, r2c, t2c, r3c, r4c
    )

    halo_start(0, feat, fmap, 0)
    halo_start(0, feat, fmap, 1)
    cot_copies = spread(
        lambda s: cot.at[:, s], lambda s: cotp.at[:, s],
        lambda k: cot_send.at[k], lambda k: cot_recv.at[k],
    )
    start(cot_copies)

    def forward(row, count, first=False, last=False):
        out = conv(cols1, w1, row * width, count * width).astype(BF16)
        hidden[pl.ds(row * width, count * width)] = out
        act = silu(out.astype(F32)).astype(BF16).astype(F32)
        build(cols2, row * width, inside(act, first, last))

    def nrm_copies(h):
        return spread(
            lambda s: normed.at[h, s], lambda s: normp.at[h, s],
            lambda k: nrm_send.at[h, k], lambda k: nrm_recv.at[h, k],
        )

    def norm(h):
        offset = h * half
        x = fmap[pl.ds(edge + offset, half)].astype(F32)
        summed = (x + conv(cols2, w2, offset, half)).astype(BF16).astype(F32)
        centred = summed - jnp.mean(summed, axis=-1, keepdims=True)
        scale = lax.rsqrt(jnp.mean(centred * centred, axis=-1, keepdims=True) + 1e-05)
        inv[h] = jnp.broadcast_to(scale, (half, 128))
        nf = centred * scale
        normed_f[h] = nf
        normed[h] = nf.astype(BF16)
        start(nrm_copies(h))
        normp[h, mine] = normed[h, mine]

    loads[0].wait()
    build(cols1, edge, silu(fmap[pl.ds(edge, pixels)].astype(F32)))
    loads[1].wait()
    forward(DEEP, rows - DEEP)
    halo_here(0, feat, fmap, 1)
    build(cols1, 0, silu(fmap[pl.ds(0, edge)].astype(F32)))
    forward(0, DEEP, first=True)
    loads[2].wait()
    norm(0)
    halo_here(0, feat, fmap, 0)
    build(cols1, edge + pixels, silu(fmap[pl.ds(edge + pixels, edge)].astype(F32)))
    forward(rows, DEEP, last=True)
    norm(1)
    mark("normed")

    for item in loads[3:]:
        item.wait()
    wait(cot_copies)
    gmix = dot_nt(cotp[...].reshape(pixels, chan), wo[...]).astype(BF16)
    ia = lax.rem(lax.broadcasted_iota(jnp.int32, (half, half), 0), share)
    ib = lax.rem(lax.broadcasted_iota(jnp.int32, (half, half), 1), share)
    same = ia == ib
    factor = chan ** (-0.5)

    def bck_copies(h):
        return spread(
            lambda s: backp.at[h, s], lambda s: gn.at[h, s],
            lambda k: bck_send.at[h, k], lambda k: bck_recv.at[h, k],
        )

    def attend(h):
        rp = normp[h]
        gm = gmix[h * half : (h + 1) * half]
        query = dot(rp, wq[...]).astype(BF16)
        key = dot(rp, wk[...]).astype(BF16)
        value = dot(rp, wv[...]).astype(BF16)
        scores = jnp.where(same, dot_nt(query, key) * factor, -jnp.inf)
        expo = jnp.exp(scores - jnp.max(scores, axis=-1, keepdims=True))
        prob_f = expo / jnp.sum(expo, axis=-1, keepdims=True)
        prob = prob_f.astype(BF16)
        grad_prob = dot_nt(gm, value)
        inner = jnp.sum(prob_f * grad_prob, axis=-1, keepdims=True)
        grad_score = (prob_f * (grad_prob - inner) * factor).astype(BF16)
        grad_value = dot_tn(prob, gm).astype(BF16)
        grad_query = dot(grad_score, key).astype(BF16)
        grad_key = dot_tn(grad_score, query).astype(BF16)
        back = (
            dot_nt(grad_query, wq[...]) + dot_nt(grad_key, wk[...]) + dot_nt(grad_value, wv[...])
        )
        backp[h] = back.astype(BF16)
        start(bck_copies(h))
        gn[h, mine] = backp[h, mine]
        gq[h] = grad_query
        gk[h] = grad_key
        gv[h] = grad_value
        mx[h] = dot(prob, value).astype(BF16)

    for h in range(CHUNKS):
        wait(nrm_copies(h))
        attend(h)
    mark("attended")
    parts = part_a.shape[3]
    unit = chan // (views * parts)
    for t, (lhs, rhs) in enumerate(((normp, gq), (normp, gk), (normp, gv), (mx, cotp))):
        term = dot_tn(
            lhs[...].reshape(pixels, chan), rhs[...].reshape(pixels, chan)
        ).astype(BF16)
        for u in range(views * parts):
            v, q = divmod(u, parts)
            part_a[0, v // 2, v % 2, q, t] = term[u * unit : (u + 1) * unit]
    launch_a()

    def backward(h):
        gnf = gn[h].astype(F32)
        nf = normed_f[h]
        gsum = cotv[h].astype(F32) + inv[h, :, 0:1] * (
            gnf
            - jnp.mean(gnf, axis=-1, keepdims=True)
            - nf * jnp.mean(gnf * nf, axis=-1, keepdims=True)
        )
        gs[h] = gsum
        g2[pl.ds(edge + h * half, half)] = gsum.astype(BF16)

    step_a(1)
    for h in range(CHUNKS):
        wait(bck_copies(h))
        backward(h)
        if h == 0:
            halo_start(1, g2, g2, 0)
    halo_start(1, g2, g2, 1)
    mark("g2")
    wgrad(cols2, 0, g2[pl.ds(edge, pixels)], part_b)
    launch_b()
    build(colsg, edge, g2[pl.ds(edge, pixels)].astype(F32))
    step_a(2)
    step_b(1)

    def flipped(row, count, first=False, last=False):
        slope = conv_flip(colsg, w2, row * width, count * width)
        own = slope * silu_slope(hidden[pl.ds(row * width, count * width)].astype(F32))
        g1[pl.ds(row * width, count * width)] = inside(own, first, last).astype(BF16)

    halo_here(1, g2, g2, 1)
    build(colsg, 0, g2[pl.ds(0, edge)].astype(F32))
    halo_here(1, g2, g2, 0)
    build(colsg, edge + pixels, g2[pl.ds(edge + pixels, edge)].astype(F32))
    flipped(0, rows + 2, True, True)
    mark("g1")
    wgrad(cols1, width, g1[pl.ds(width, pixels)], part_c)
    launch_c()
    build(colsg, 0, g1[...].astype(F32))
    step_c(1)
    step_b(2)
    slope = conv_flip(colsg, w1, 0, pixels)
    gfeat[...] = (
        gs[...].reshape(pixels, chan)
        + slope * silu_slope(fmap[pl.ds(edge, pixels)].astype(F32))
    ).astype(BF16)
    step_a(3)
    step_c(2)
    step_b(3)
    step_c(3)

    for way in range(2):
        halo_sent(0, feat, fmap, way)
        halo_sent(1, g2, g2, way)

    def store_a(u, value):
        attn_out[:, pl.ds(u * unit, unit), :] = value.astype(attn_out.dtype)

    def store_conv(i):
        def store(u, value):
            size = value.shape[0]
            conv_out[i, pl.ds(u * size, size), :] = value.astype(conv_out.dtype)

        return store

    finish_a(store_a)
    finish_b(store_conv(1))
    finish_c(store_conv(0))


def run_full(
    dims, feat, cot, w1h, w2h, wqh, wkh, wvh, woh, gfeat, conv_out, attn_out,
    w1, w2, wq, wk, wv, wo, load,
    fmap, cotv, cols1, cols2, colsg, hidden, normed, normed_f, inv, g2, gs, g1, acc,
    normp, cotp, backp, gn, gq, gk, gv, mx,
    part_a, part_b, part_c, r1a, r1b, r1c, t1a, r2a,
    t2a, t2b, t2c, r3a, r3b, r3c, r4a, r4b, r4c,
    near_send, near_recv, swap_send, swap_recv,
    cot_send, cot_recv, nrm_send, nrm_recv, bck_send, bck_recv,
    s1_send, s1_recv, s2_send, s2_recv, s3_send, s3_recv, s4_send, s4_recv,
):
    views, strips, rows, width, chan = dims
    pixels = rows * width
    half = pixels // CHUNKS
    block = rows // CHUNKS
    share = half // views
    every = strips * pixels
    lanes = chan // strips
    zs = views // 2
    view = lax.axis_index("view")
    strip = lax.axis_index("strip")
    core = lax.rem(view, 2)
    zed = lax.div(view, 2)
    other = 1 - strip
    mine = pl.ds(pl.multiple_of(view * share, share), share)
    columns = pl.ds(pl.multiple_of(strip * lanes, lanes), lanes)

    def span(row, count):
        return pl.ds(pl.multiple_of(row * width, width), count * width)

    barrier = pltpu.get_barrier_semaphore()
    for k in range(1, views):
        pl.semaphore_signal(
            barrier, inc=1, device_id={"view": lax.rem(view + k, views)}, device_id_type=MESH
        )
    pl.semaphore_signal(barrier, inc=1, device_id={"strip": other}, device_id_type=MESH)
    loads = [
        pltpu.make_async_copy(src, dst, load.at[i])
        for i, (src, dst) in enumerate(
            (
                (feat, fmap.at[span(strip * rows, rows)]),
                (w1h, w1), (w2h, w2), (woh, wo), (wqh, wq), (wkh, wk), (wvh, wv), (cot, cotv),
            )
        )
    ]
    for item in loads:
        item.start()
    for cols in (cols1, cols2, colsg):
        cols[pl.ds(0, width)] = jnp.zeros((width, 3 * chan), BF16)
        cols[pl.ds(width + every, width)] = jnp.zeros((width, 3 * chan), BF16)
    g1[pl.ds(0, width)] = jnp.zeros((width, chan), BF16)
    g1[pl.ds(width + every, width)] = jnp.zeros((width, chan), BF16)
    pl.semaphore_wait(barrier, views)

    def start(copies):
        for copy in copies:
            copy.start()

    def wait(copies):
        for copy in copies:
            copy.wait()

    def first(h, which):
        return which * (3 * block) if h == 0 else block * (1 + which)

    def near_copies(h):
        place = span(first(h, strip), block)
        inside = span(first(h, strip) - strip * rows, block)
        return [
            pltpu.make_async_remote_copy(
                src_ref=feat.at[inside], dst_ref=fmap.at[place],
                send_sem=near_send.at[h], recv_sem=near_recv.at[h],
                device_id={"strip": other}, device_id_type=MESH,
            )
        ]

    def swap_copies(h):
        place = span(first(h, strip), block)
        return [
            pltpu.make_async_remote_copy(
                src_ref=g2.at[place], dst_ref=g2.at[place],
                send_sem=swap_send.at[h], recv_sem=swap_recv.at[h],
                device_id={"strip": other}, device_id_type=MESH,
            )
        ]

    def spread(src, dst, send, recv):
        out = []
        for k in range(1, views):
            peer = lax.rem(view + k, views)
            out.append(
                pltpu.make_async_remote_copy(
                    src_ref=src(pl.ds(pl.multiple_of(peer * share, share), share)),
                    dst_ref=dst(mine),
                    send_sem=send(k), recv_sem=recv(k),
                    device_id={"view": peer}, device_id_type=MESH,
                )
            )
        return out

    def from_cot(h, s):
        place = first(h, strip) - strip * rows
        return pl.ds(pl.multiple_of(place * width + s.start, share), share)

    def cot_copies(h):
        return spread(
            lambda s: cot.at[from_cot(h, s)], lambda s: cotp.at[h, s],
            lambda k: cot_send.at[h, k], lambda k: cot_recv.at[h, k],
        )

    def nrm_copies(h):
        return spread(
            lambda s: normed.at[h, s], lambda s: normp.at[h, s],
            lambda k: nrm_send.at[h, k], lambda k: nrm_recv.at[h, k],
        )

    def bck_copies(h):
        return spread(
            lambda s: backp.at[h, s], lambda s: gn.at[h, s],
            lambda k: bck_send.at[h, k], lambda k: bck_recv.at[h, k],
        )

    def build(cols, row, x):
        count = x.shape[0]
        place = span(row, count // width)
        column = lax.rem(lax.broadcasted_iota(jnp.int32, (count, chan), 0), width)
        left = jnp.where(column == 0, 0.0, pltpu.roll(x, 1, 0))
        right = jnp.where(column == width - 1, 0.0, pltpu.roll(x, count - 1, 0))
        cols[place, pl.ds(0, chan)] = left.astype(BF16)
        cols[place, pl.ds(chan, chan)] = x.astype(BF16)
        cols[place, pl.ds(2 * chan, chan)] = right.astype(BF16)

    def conv(cols, w, row, count):
        total = None
        for r in range(3):
            term = dot(cols[span(row + r, count), :], w[r])
            total = term if total is None else total + term
        return total

    def conv_flip(cols, w, row, count):
        total = None
        for r in range(3):
            for s in range(3):
                term = dot_nt(
                    cols[span(row + r, count), pl.ds(s * chan, chan)],
                    w[2 - r, pl.ds((2 - s) * chan, chan), :],
                )
                total = term if total is None else total + term
        return total

    def scatter(r, value, out):
        pieces, _, _, _, unit, _ = out.shape
        per = 3 * chan // unit
        for m in range(per):
            v, p = divmod(r * per + m, pieces)
            out[p, v // 2, v % 2, 0] = value[m * unit : (m + 1) * unit].astype(BF16)

    sems = (s1_send, s1_recv, s2_send, s2_recv, s3_send, s3_recv, s4_send, s4_recv)
    place = (view, strip, core, zed, views, strips, zs)
    count_a = part_a.shape[0]
    count_b = part_b.shape[0]
    launch_a, step_a, finish_a = group(
        place, sems, start, wait, 0, part_a, r1a, t1a, r2a, t2a, r3a, r4a
    )
    launch_b, step_b, finish_b = group(
        place, sems, start, wait, count_a, part_b, r1b, None, None, t2b, r3b, r4b
    )
    launch_c, step_c, finish_c = group(
        place, sems, start, wait, count_a + count_b, part_c, r1c, None, None, t2c, r3c, r4c
    )

    start(cot_copies(0))
    start(near_copies(1))
    start(near_copies(0))

    def forward(row, count):
        out = conv(cols1, w1, row, count).astype(BF16)
        hidden[span(row, count)] = out
        build(cols2, row + 1, silu(out.astype(F32)).astype(BF16).astype(F32))

    def columns_of(row, count):
        build(cols1, row + 1, silu(fmap[span(row, count)].astype(F32)))

    def norm(h):
        row = first(h, strip)
        x = fmap[span(row, block)].astype(F32)
        summed = (x + conv(cols2, w2, row, block)).astype(BF16).astype(F32)
        centred = summed - jnp.mean(summed, axis=-1, keepdims=True)
        scale = lax.rsqrt(jnp.mean(centred * centred, axis=-1, keepdims=True) + 1e-05)
        inv[h] = jnp.broadcast_to(scale, (half, 128))
        nf = centred * scale
        normed_f[h] = nf
        normed[h] = nf.astype(BF16)
        start(nrm_copies(h))
        normp[h, mine] = normed[h, mine]

    loads[0].wait()
    columns_of(strip * rows, rows)
    loads[1].wait()
    forward((rows + 1) * strip, rows - 1)
    loads[2].wait()
    norm(0)
    start(cot_copies(1))
    mark("norm0")
    wait(near_copies(1))
    columns_of(first(1, other), block)
    forward(rows - 1, 2)
    norm(1)
    mark("norm1")
    wait(near_copies(0))
    columns_of(first(0, other), block)
    forward((rows + 1) * other, rows - 1)
    for item in loads[3:]:
        item.wait()
    mark("forward")

    ia = lax.rem(lax.broadcasted_iota(jnp.int32, (half, half), 0), share)
    ib = lax.rem(lax.broadcasted_iota(jnp.int32, (half, half), 1), share)
    same = ia == ib
    factor = chan ** (-0.5)

    def attend(h):
        rp = normp[h]
        query = dot(rp, wq[...]).astype(BF16)
        key = dot(rp, wk[...]).astype(BF16)
        value = dot(rp, wv[...]).astype(BF16)
        scores = jnp.where(same, dot_nt(query, key) * factor, -jnp.inf)
        expo = jnp.exp(scores - jnp.max(scores, axis=-1, keepdims=True))
        prob_f = expo / jnp.sum(expo, axis=-1, keepdims=True)
        prob = prob_f.astype(BF16)
        gm = dot_nt(cotp[h], wo[...]).astype(BF16)
        grad_prob = dot_nt(gm, value)
        inner = jnp.sum(prob_f * grad_prob, axis=-1, keepdims=True)
        grad_score = (prob_f * (grad_prob - inner) * factor).astype(BF16)
        grad_value = dot_tn(prob, gm).astype(BF16)
        grad_query = dot(grad_score, key).astype(BF16)
        grad_key = dot_tn(grad_score, query).astype(BF16)
        back = (
            dot_nt(grad_query, wq[...]) + dot_nt(grad_key, wk[...]) + dot_nt(grad_value, wv[...])
        )
        backp[h] = back.astype(BF16)
        start(bck_copies(h))
        gn[h, mine] = backp[h, mine]
        gq[h] = grad_query
        gk[h] = grad_key
        gv[h] = grad_value
        mx[h] = dot(prob, value).astype(BF16)

    for h in range(CHUNKS):
        wait(cot_copies(h))
        cotp[h, mine] = cotv[from_cot(h, mine)]
        wait(nrm_copies(h))
        attend(h)
        mark("attend%d" % h)
    parts = part_a.shape[3]
    unit = chan // (views * parts)
    for t, (lhs, rhs) in enumerate(((normp, gq), (normp, gk), (normp, gv), (mx, cotp))):
        term = dot_tn(
            lhs[...].reshape(pixels, chan), rhs[...].reshape(pixels, chan)
        ).astype(BF16)
        for u in range(views * parts):
            v, q = divmod(u, parts)
            part_a[0, v // 2, v % 2, q, t] = term[u * unit : (u + 1) * unit]
    launch_a()
    mark("launch_a")

    def backward(h):
        row = first(h, strip)
        gnf = gn[h].astype(F32)
        nf = normed_f[h]
        gsum = cotv[span(row - strip * rows, block)].astype(F32) + inv[h, :, 0:1] * (
            gnf
            - jnp.mean(gnf, axis=-1, keepdims=True)
            - nf * jnp.mean(gnf * nf, axis=-1, keepdims=True)
        )
        gs[span(row - strip * rows, block)] = gsum
        g2[span(row, block)] = gsum.astype(BF16)
        start(swap_copies(h))
        build(colsg, row + 1, g2[span(row, block)].astype(F32))

    wait(bck_copies(0))
    backward(0)
    step_a(1)
    wait(bck_copies(1))
    backward(1)
    mark("backward")
    for r in range(3):
        acc[r] = dot_tn(
            cols2[span(strip * rows + r, rows)], g2[span(strip * rows, rows), columns]
        )
    step_a(2)
    for h in range(CHUNKS):
        wait(swap_copies(h))
        row = first(h, other)
        build(colsg, row + 1, g2[span(row, block)].astype(F32))
    mark("swapped")
    for r in range(3):
        term = dot_tn(cols2[span(other * rows + r, rows)], g2[span(other * rows, rows), columns])
        scatter(r, acc[r] + term, part_b)
    launch_b()
    mark("launch_b")
    slope = conv_flip(colsg, w2, 0, strips * rows)
    g1[pl.ds(width, every)] = (slope * silu_slope(hidden[...].astype(F32))).astype(BF16)
    step_b(1)
    for r in range(3):
        scatter(r, dot_tn(cols1[pl.ds(r * width, every)], g1[pl.ds(width, every), columns]), part_c)
    launch_c()
    mark("launch_c")
    build(colsg, 0, g1[span(strip * rows, rows + 2)].astype(F32))
    step_c(1)
    slope = conv_flip(colsg, w1, 0, rows)
    gfeat[...] = (
        gs[...] + slope * silu_slope(fmap[span(strip * rows, rows)].astype(F32))
    ).astype(BF16)
    mark("gfeat")
    step_a(3)
    step_b(2)
    mark("step_b2")
    step_c(2)
    mark("step_c2")

    def store_a(u, value):
        attn_out[:, pl.ds(u * unit, unit), :] = value.astype(attn_out.dtype)

    def store_conv(i):
        def store(u, value):
            p, t = divmod(u, strips)
            size = value.shape[0]
            conv_out[i, pl.ds(p * size, size), pl.ds(t * lanes, lanes)] = value.astype(
                conv_out.dtype
            )

        return store

    finish_a(store_a)
    finish_b(store_conv(1))
    finish_c(store_conv(0))


def widen(a, b, c, x, y, z):
    x[...] = a[...]
    y[...] = b[...].astype(F32)
    z[...] = c[...].astype(F32)


def body(features, cotangent, conv_first, conv_second, w_query, w_key, w_value, w_out):
    views = lax.axis_size("view")
    strips = lax.axis_size("strip")
    _, rows, width, chan = features.shape
    pixels = rows * width
    zs = views // 2
    cut = 9 * chan // views
    slab = chan // views
    vm = pltpu.VMEM
    dma = pltpu.SemaphoreType.DMA
    flat = (pixels, chan)
    split = (CHUNKS, pixels // CHUNKS, chan)
    wide = (rows + 2 * DEEP) * width
    near = (rows + 2) * width
    exact = cut % (16 * strips) == 0 and slab % (16 * strips) == 0
    parts = strips if exact else 1
    pieces = 3 if cut % (48 * parts) == 0 else 1
    full = strips == 2 and exact and pieces == 3 and rows == 2 * DEEP and chan % 256 == 0
    conv_u = (cut // (parts * pieces), chan)
    attn_u = (4, slab // parts, chan)
    units = ((1, attn_u), (pieces, conv_u), (pieces, conv_u))
    total = 1 + 2 * pieces
    hold = {
        "part_": [(n, zs, 2, parts) + u for n, u in units],
        "r1": [(n, zs, parts) + u for n, u in units],
        "t1": [(n, parts, zs) + u for n, u in units],
        "r2": [(n, max(parts - 1, 1), zs) + u for n, u in units],
        "t2": [(n, zs) + u for n, u in units],
        "r3": [(n, zs - 1) + u for n, u in units],
        "r4": [(n, strips) + u for n, u in units],
    }
    conv_k = (3, 3 * chan, chan)
    square = (chan, chan)
    scratch = {
        "w1": vm(conv_k, BF16), "w2": vm(conv_k, BF16),
        "wq": vm(square, BF16), "wk": vm(square, BF16),
        "wv": vm(square, BF16), "wo": vm(square, BF16), "load": dma((9,)),
        "fmap": vm((wide, chan), BF16), "cotv": vm(split, BF16),
        "cols1": vm((wide, 3 * chan), BF16), "cols2": vm((near, 3 * chan), BF16),
        "colsg": vm((wide, 3 * chan), BF16),
        "hidden": vm((near, chan), BF16), "normed": vm(split, BF16), "normed_f": vm(split, F32),
        "inv": vm(split[:2] + (128,), F32), "g2": vm((wide, chan), BF16), "gs": vm(split, F32),
        "g1": vm((near, chan), BF16),
    }
    for name in ("normp", "cotp", "backp", "gn", "gq", "gk", "gv", "mx"):
        scratch[name] = vm(split, BF16)
    for name, shapes in hold.items():
        for letter, shape in zip("abc", shapes):
            scratch[name + letter] = vm(shape, BF16)
    if full:
        conv_u = (cut // pieces, chan // strips)
        for letter in "bc":
            scratch["part_" + letter] = vm((pieces, zs, 2, 1) + conv_u, BF16)
            scratch["r1" + letter] = vm((pieces, zs, 1) + conv_u, BF16)
            scratch["t2" + letter] = vm((pieces, zs) + conv_u, BF16)
            scratch["r3" + letter] = vm((pieces, zs - 1) + conv_u, BF16)
            scratch["r4" + letter] = vm((pieces, strips) + conv_u, BF16)
            del scratch["t1" + letter], scratch["r2" + letter]
        padded = (strips * rows + 2) * width
        for name in ("cols1", "cols2", "colsg"):
            scratch[name] = vm((padded, 3 * chan), BF16)
        for name in ("fmap", "hidden", "g2"):
            scratch[name] = vm((strips * pixels, chan), BF16)
        scratch["g1"] = vm((padded, chan), BF16)
        scratch["cotv"] = vm(flat, BF16)
        scratch["gs"] = vm(flat, F32)
        scratch["acc"] = vm((3, 3 * chan, chan // strips), F32)
    counts = {
        "halo": (2, 2), "cot": (views,), "nrm": (CHUNKS, views), "bck": (CHUNKS, views),
        "s1": (total,), "s2": (total, strips), "s3": (total, zs), "s4": (total, strips),
    }
    if full:
        del counts["halo"]
        counts["near"] = counts["swap"] = (CHUNKS,)
        counts["cot"] = (CHUNKS, views)
    for name, shape in counts.items():
        scratch[name + "_send"] = dma(shape)
        scratch[name + "_recv"] = dma(shape)
    names = (
        "feat", "cot", "w1h", "w2h", "wqh", "wkh", "wvh", "woh", "gfeat", "conv_out", "attn_out",
    ) + tuple(scratch)
    spec = pl.BlockSpec(memory_space=pltpu.VMEM)
    stay = pl.BlockSpec(memory_space=pl.ANY)
    kind = BF16 if exact else F32
    conv_s = (2, cut, chan)
    attn_s = (4, slab, chan)
    outs = pl.pallas_call(
        functools.partial(
            kernel, run_full if full else run, (views, strips, rows, width, chan), names
        ),
        out_shape=(
            jax.ShapeDtypeStruct(flat, BF16),
            jax.ShapeDtypeStruct(conv_s, kind),
            jax.ShapeDtypeStruct(attn_s, kind),
        ),
        in_specs=[stay] * 8,
        out_specs=(spec, spec, spec),
        scratch_shapes=list(scratch.values()),
        compiler_params=pltpu.CompilerParams(
            collective_id=0, has_side_effects=True, vmem_limit_bytes=56 * 1024 * 1024
        ),
    )(
        features.reshape(flat),
        cotangent.reshape(flat if full else split),
        conv_first.reshape(3, 3 * chan, chan),
        conv_second.reshape(3, 3 * chan, chan),
        w_query, w_key, w_value, w_out,
    )
    outs = pl.pallas_call(
        widen,
        out_shape=(
            jax.ShapeDtypeStruct(flat, BF16),
            jax.ShapeDtypeStruct(conv_s, F32),
            jax.ShapeDtypeStruct(attn_s, F32),
        ),
        in_specs=[spec] * 3,
        out_specs=(spec, spec, spec),
    )(*outs)
    return (outs[0].reshape(features.shape), outs[1], outs[2])


def solution(mesh):
    rows = P(("orbit", "view"), "strip", None, None)
    grads = P("orbit", "view", None)
    return jax.shard_map(
        body,
        mesh=mesh,
        in_specs=(rows, rows, P(), P(), P(), P(), P(), P()),
        out_specs=(rows, grads, grads),
        check_vma=False,
    )
```

```python
import functools

import jax
import jax.numpy as jnp
from jax import lax
from jax.experimental import pallas as pl
from jax.experimental.pallas import tpu as pltpu
from jax.sharding import PartitionSpec as P

MESH = pl.DeviceIdType.MESH
F32 = jnp.float32
BF16 = jnp.bfloat16
NT = (((1,), (1,)), ((), ()))
TN = (((0,), (0,)), ((), ()))
CHUNKS = 2
DEEP = 2
SPLIT = 1


def dot(a, b):
    return jnp.dot(a, b, preferred_element_type=F32)


def dot_nt(a, b):
    return lax.dot_general(a, b, NT, preferred_element_type=F32)


def dot_tn(a, b):
    return lax.dot_general(a, b, TN, preferred_element_type=F32)


def silu(x):
    return x * jax.nn.sigmoid(x)


def silu_slope(x):
    sigma = jax.nn.sigmoid(x)
    return sigma * (1.0 + x * (1.0 - sigma))


def group(place, sems, start, wait, base, part, r1, t1, r2, t2, r3, r4, split=False):
    view, strip, core, zed, views, strips, zs = place
    s1_send, s1_recv, s2_send, s2_recv, s3_send, s3_recv, s4_send, s4_recv = sems
    parts = part.shape[3]
    shares = split or parts > 1

    def stage1(p):
        return [
            pltpu.make_async_remote_copy(
                src_ref=part.at[p, :, 1 - core], dst_ref=r1.at[p],
                send_sem=s1_send.at[base + p], recv_sem=s1_recv.at[base + p],
                device_id={"view": view + 1 - 2 * core}, device_id_type=MESH,
            )
        ]

    def reduce1(p):
        for j in range(zs):
            if t1 is None:
                t2[p, j] = (
                    part[p, j, core, 0].astype(F32) + r1[p, j, 0].astype(F32)
                ).astype(BF16)
                continue
            for t in range(parts):
                t1[p, t, j] = (
                    part[p, j, core, t].astype(F32) + r1[p, j, t].astype(F32)
                ).astype(BF16)

    def stage2(p):
        out = []
        for k in range(1, parts):
            other = lax.rem(strip + k, strips)
            out.append(
                pltpu.make_async_remote_copy(
                    src_ref=t1.at[p, other], dst_ref=r2.at[p, k - 1],
                    send_sem=s2_send.at[base + p, k], recv_sem=s2_recv.at[base + p, k],
                    device_id={"strip": other}, device_id_type=MESH,
                )
            )
        return out

    def reduce2(p):
        own = strip if parts > 1 else 0
        for j in range(zs):
            value = t1[p, own, j].astype(F32)
            for k in range(1, parts):
                value = value + r2[p, k - 1, j].astype(F32)
            t2[p, j] = value.astype(BF16)

    def stage3(p):
        out = []
        for k in range(1, zs):
            other = lax.rem(zed + k, zs)
            out.append(
                pltpu.make_async_remote_copy(
                    src_ref=t2.at[p, other], dst_ref=r3.at[p, k - 1],
                    send_sem=s3_send.at[base + p, k], recv_sem=s3_recv.at[base + p, k],
                    device_id={"view": other * 2 + core}, device_id_type=MESH,
                )
            )
        return out

    def reduce3(p):
        value = t2[p, zed].astype(F32)
        for k in range(1, zs):
            value = value + r3[p, k - 1].astype(F32)
        r4[p, strip] = value.astype(BF16)

    def stage4(p):
        out = []
        for k in range(1, strips):
            out.append(
                pltpu.make_async_remote_copy(
                    src_ref=r4.at[p, strip], dst_ref=r4.at[p, strip],
                    send_sem=s4_send.at[base + p, k], recv_sem=s4_recv.at[base + p, k],
                    device_id={"strip": lax.rem(strip + k, strips)}, device_id_type=MESH,
                )
            )
        return out

    def final(p):
        if shares:
            return [r4[p, t].astype(F32) for t in range(strips)]
        value = r4[p, 0].astype(F32)
        for t in range(1, strips):
            value = value + r4[p, t].astype(F32)
        return [value]

    reduces = (None, reduce1, reduce2, reduce3)
    stages = (stage1, stage2, stage3, stage4)
    if t1 is None:
        reduces = (None, reduce1, reduce3)
        stages = (stage1, stage3, stage4)

    def launch():
        for p in range(part.shape[0]):
            start(stage1(p))

    def advance(k, p):
        wait(stages[k - 1](p))
        reduces[k](p)
        start(stages[k](p))

    def advance_all(k):
        for p in range(part.shape[0]):
            advance(k, p)

    def finish(store):
        for p in range(part.shape[0]):
            wait(stage4(p))
            for t, value in enumerate(final(p)):
                store(p * (strips if shares else 1) + t, value)

    return launch, advance_all, finish


def mark(name):
    pass


def kernel(call, dims, names, *refs):
    call(dims, **dict(zip(names, refs, strict=True)))


def run(
    dims, feat, cot, w1h, w2h, wqh, wkh, wvh, woh, gfeat, conv_out, attn_out,
    w1, w2, wq, wk, wv, wo, load,
    fmap, cotv, cols1, cols2, colsg, hidden, normed, normed_f, inv, g2, gs, g1,
    normp, cotp, backp, gn, gq, gk, gv, mx,
    part_a, part_b, part_c, r1a, r1b, r1c, t1a, t1b, t1c, r2a, r2b, r2c,
    t2a, t2b, t2c, r3a, r3b, r3c, r4a, r4b, r4c,
    halo_send, halo_recv, cot_send, cot_recv, nrm_send, nrm_recv, bck_send, bck_recv,
    s1_send, s1_recv, s2_send, s2_recv, s3_send, s3_recv, s4_send, s4_recv,
):
    views, strips, rows, width, chan = dims
    pixels = rows * width
    half = pixels // CHUNKS
    share = half // views
    edge = DEEP * width
    zs = views // 2
    view = lax.axis_index("view")
    strip = lax.axis_index("strip")
    core = lax.rem(view, 2)
    zed = lax.div(view, 2)

    barrier = pltpu.get_barrier_semaphore()
    for k in range(1, views):
        pl.semaphore_signal(
            barrier, inc=1, device_id={"view": lax.rem(view + k, views)}, device_id_type=MESH
        )
    for k in range(1, strips):
        pl.semaphore_signal(
            barrier, inc=1, device_id={"strip": lax.rem(strip + k, strips)}, device_id_type=MESH
        )
    mine = pl.ds(pl.multiple_of(view * share, share), share)
    loads = [
        pltpu.make_async_copy(src, dst, load.at[i])
        for i, (src, dst) in enumerate(
            (
                (feat, fmap.at[pl.ds(edge, pixels)]),
                (w1h, w1), (w2h, w2), (woh, wo), (wqh, wq), (wkh, wk), (wvh, wv),
                (cot.at[:, mine], cotp.at[:, mine]), (cot, cotv),
            )
        )
    ]
    for item in loads:
        item.start()

    @pl.when(strip == 0)
    def _():
        fmap[pl.ds(0, edge)] = jnp.zeros((edge, chan), BF16)
        g2[pl.ds(0, edge)] = jnp.zeros((edge, chan), BF16)

    @pl.when(strip == strips - 1)
    def _():
        fmap[pl.ds(edge + pixels, edge)] = jnp.zeros((edge, chan), BF16)
        g2[pl.ds(edge + pixels, edge)] = jnp.zeros((edge, chan), BF16)

    pl.semaphore_wait(barrier, views - 1 + strips - 1)

    def halo_copy(e, src, dst, way):
        start = 0 if way == 0 else pixels - edge
        land = edge + pixels if way == 0 else 0
        near = lax.max(strip - 1, 0) if way == 0 else lax.min(strip + 1, strips - 1)
        base = edge if src is dst else 0
        return pltpu.make_async_remote_copy(
            src_ref=src.at[pl.ds(base + start, edge)], dst_ref=dst.at[pl.ds(land, edge)],
            send_sem=halo_send.at[e, way], recv_sem=halo_recv.at[e, way],
            device_id={"strip": near}, device_id_type=MESH,
        )

    def halo_start(e, src, dst, way):
        copy = halo_copy(e, src, dst, way)
        pl.when(strip > 0 if way == 0 else strip < strips - 1)(copy.start)

    def halo_sent(e, src, dst, way):
        copy = halo_copy(e, src, dst, way)
        pl.when(strip > 0 if way == 0 else strip < strips - 1)(copy.wait_send)

    def halo_here(e, src, dst, way):
        copy = halo_copy(e, src, dst, way)
        pl.when(strip < strips - 1 if way == 0 else strip > 0)(copy.wait_recv)

    def spread(src, dst, send, recv):
        out = []
        for k in range(1, views):
            peer = lax.rem(view + k, views)
            out.append(
                pltpu.make_async_remote_copy(
                    src_ref=src(pl.ds(pl.multiple_of(peer * share, share), share)),
                    dst_ref=dst(mine),
                    send_sem=send(k), recv_sem=recv(k),
                    device_id={"view": peer}, device_id_type=MESH,
                )
            )
        return out

    def start(copies):
        for copy in copies:
            copy.start()

    def wait(copies):
        for copy in copies:
            copy.wait()

    def build(cols, offset, x):
        count = x.shape[0]
        column = lax.rem(lax.broadcasted_iota(jnp.int32, (count, chan), 0), width)
        left = jnp.where(column == 0, 0.0, pltpu.roll(x, 1, 0))
        right = jnp.where(column == width - 1, 0.0, pltpu.roll(x, count - 1, 0))
        cols[pl.ds(offset, count), pl.ds(0, chan)] = left.astype(BF16)
        cols[pl.ds(offset, count), pl.ds(chan, chan)] = x.astype(BF16)
        cols[pl.ds(offset, count), pl.ds(2 * chan, chan)] = right.astype(BF16)

    def conv(cols, w, offset, count):
        total = None
        for r in range(3):
            term = dot(cols[pl.ds(offset + r * width, count), :], w[r])
            total = term if total is None else total + term
        return total

    def conv_flip(cols, w, offset, count):
        total = None
        for r in range(3):
            for s in range(3):
                term = dot_nt(
                    cols[pl.ds(offset + r * width, count), pl.ds(s * chan, chan)],
                    w[2 - r, pl.ds((2 - s) * chan, chan), :],
                )
                total = term if total is None else total + term
        return total

    def wgrad(cols, offset, d, out):
        pieces, _, _, parts, unit, _ = out.shape
        per = 3 * chan // unit
        for r in range(3):
            value = dot_tn(cols[pl.ds(offset + r * width, pixels), :], d).astype(BF16)
            for m in range(per):
                u = r * per + m
                v, rest = divmod(u, pieces * parts)
                p, t = divmod(rest, parts)
                out[p, v // 2, v % 2, t] = value[m * unit : (m + 1) * unit]

    def inside(x, first, last):
        if first:
            low = lax.broadcasted_iota(jnp.int32, x.shape, 0)
            x = jnp.where(jnp.logical_and(low < width, strip == 0), 0.0, x)
        if last:
            high = lax.broadcasted_iota(jnp.int32, x.shape, 0)
            gone = jnp.logical_and(high >= x.shape[0] - width, strip == strips - 1)
            x = jnp.where(gone, 0.0, x)
        return x

    sems = (s1_send, s1_recv, s2_send, s2_recv, s3_send, s3_recv, s4_send, s4_recv)
    place = (view, strip, core, zed, views, strips, zs)
    count_a = part_a.shape[0]
    count_b = part_b.shape[0]
    launch_a, step_a, finish_a = group(
        place, sems, start, wait, 0, part_a, r1a, t1a, r2a, t2a, r3a, r4a
    )
    launch_b, step_b, finish_b = group(
        place, sems, start, wait, count_a, part_b, r1b, t1b, r2b, t2b, r3b, r4b
    )
    launch_c, step_c, finish_c = group(
        place, sems, start, wait, count_a + count_b, part_c, r1c, t1c, r2c, t2c, r3c, r4c
    )

    halo_start(0, feat, fmap, 0)
    halo_start(0, feat, fmap, 1)
    cot_copies = spread(
        lambda s: cot.at[:, s], lambda s: cotp.at[:, s],
        lambda k: cot_send.at[k], lambda k: cot_recv.at[k],
    )
    start(cot_copies)

    def forward(row, count, first=False, last=False):
        out = conv(cols1, w1, row * width, count * width).astype(BF16)
        hidden[pl.ds(row * width, count * width)] = out
        act = silu(out.astype(F32)).astype(BF16).astype(F32)
        build(cols2, row * width, inside(act, first, last))

    def nrm_copies(h):
        return spread(
            lambda s: normed.at[h, s], lambda s: normp.at[h, s],
            lambda k: nrm_send.at[h, k], lambda k: nrm_recv.at[h, k],
        )

    def norm(h):
        offset = h * half
        x = fmap[pl.ds(edge + offset, half)].astype(F32)
        summed = (x + conv(cols2, w2, offset, half)).astype(BF16).astype(F32)
        centred = summed - jnp.mean(summed, axis=-1, keepdims=True)
        scale = lax.rsqrt(jnp.mean(centred * centred, axis=-1, keepdims=True) + 1e-05)
        inv[h] = jnp.broadcast_to(scale, (half, 128))
        nf = centred * scale
        normed_f[h] = nf
        normed[h] = nf.astype(BF16)
        start(nrm_copies(h))
        normp[h, mine] = normed[h, mine]

    loads[0].wait()
    build(cols1, edge, silu(fmap[pl.ds(edge, pixels)].astype(F32)))
    loads[1].wait()
    forward(DEEP, rows - DEEP)
    halo_here(0, feat, fmap, 1)
    build(cols1, 0, silu(fmap[pl.ds(0, edge)].astype(F32)))
    forward(0, DEEP, first=True)
    loads[2].wait()
    norm(0)
    halo_here(0, feat, fmap, 0)
    build(cols1, edge + pixels, silu(fmap[pl.ds(edge + pixels, edge)].astype(F32)))
    forward(rows, DEEP, last=True)
    norm(1)
    mark("normed")

    for item in loads[3:]:
        item.wait()
    wait(cot_copies)
    gmix = dot_nt(cotp[...].reshape(pixels, chan), wo[...]).astype(BF16)
    ia = lax.rem(lax.broadcasted_iota(jnp.int32, (half, half), 0), share)
    ib = lax.rem(lax.broadcasted_iota(jnp.int32, (half, half), 1), share)
    same = ia == ib
    factor = chan ** (-0.5)

    def bck_copies(h):
        return spread(
            lambda s: backp.at[h, s], lambda s: gn.at[h, s],
            lambda k: bck_send.at[h, k], lambda k: bck_recv.at[h, k],
        )

    def attend(h):
        rp = normp[h]
        gm = gmix[h * half : (h + 1) * half]
        query = dot(rp, wq[...]).astype(BF16)
        key = dot(rp, wk[...]).astype(BF16)
        value = dot(rp, wv[...]).astype(BF16)
        scores = jnp.where(same, dot_nt(query, key) * factor, -jnp.inf)
        expo = jnp.exp(scores - jnp.max(scores, axis=-1, keepdims=True))
        prob_f = expo / jnp.sum(expo, axis=-1, keepdims=True)
        prob = prob_f.astype(BF16)
        grad_prob = dot_nt(gm, value)
        inner = jnp.sum(prob_f * grad_prob, axis=-1, keepdims=True)
        grad_score = (prob_f * (grad_prob - inner) * factor).astype(BF16)
        grad_value = dot_tn(prob, gm).astype(BF16)
        grad_query = dot(grad_score, key).astype(BF16)
        grad_key = dot_tn(grad_score, query).astype(BF16)
        back = (
            dot_nt(grad_query, wq[...]) + dot_nt(grad_key, wk[...]) + dot_nt(grad_value, wv[...])
        )
        backp[h] = back.astype(BF16)
        start(bck_copies(h))
        gn[h, mine] = backp[h, mine]
        gq[h] = grad_query
        gk[h] = grad_key
        gv[h] = grad_value
        mx[h] = dot(prob, value).astype(BF16)

    for h in range(CHUNKS):
        wait(nrm_copies(h))
        attend(h)
    mark("attended")
    parts = part_a.shape[3]
    unit = chan // (views * parts)
    for t, (lhs, rhs) in enumerate(((normp, gq), (normp, gk), (normp, gv), (mx, cotp))):
        term = dot_tn(
            lhs[...].reshape(pixels, chan), rhs[...].reshape(pixels, chan)
        ).astype(BF16)
        for u in range(views * parts):
            v, q = divmod(u, parts)
            part_a[0, v // 2, v % 2, q, t] = term[u * unit : (u + 1) * unit]
    launch_a()

    def backward(h):
        gnf = gn[h].astype(F32)
        nf = normed_f[h]
        gsum = cotv[h].astype(F32) + inv[h, :, 0:1] * (
            gnf
            - jnp.mean(gnf, axis=-1, keepdims=True)
            - nf * jnp.mean(gnf * nf, axis=-1, keepdims=True)
        )
        gs[h] = gsum
        g2[pl.ds(edge + h * half, half)] = gsum.astype(BF16)

    step_a(1)
    for h in range(CHUNKS):
        wait(bck_copies(h))
        backward(h)
        if h == 0:
            halo_start(1, g2, g2, 0)
    halo_start(1, g2, g2, 1)
    mark("g2")
    wgrad(cols2, 0, g2[pl.ds(edge, pixels)], part_b)
    launch_b()
    build(colsg, edge, g2[pl.ds(edge, pixels)].astype(F32))
    step_a(2)
    step_b(1)

    def flipped(row, count, first=False, last=False):
        slope = conv_flip(colsg, w2, row * width, count * width)
        own = slope * silu_slope(hidden[pl.ds(row * width, count * width)].astype(F32))
        g1[pl.ds(row * width, count * width)] = inside(own, first, last).astype(BF16)

    halo_here(1, g2, g2, 1)
    build(colsg, 0, g2[pl.ds(0, edge)].astype(F32))
    halo_here(1, g2, g2, 0)
    build(colsg, edge + pixels, g2[pl.ds(edge + pixels, edge)].astype(F32))
    flipped(0, rows + 2, True, True)
    mark("g1")
    wgrad(cols1, width, g1[pl.ds(width, pixels)], part_c)
    launch_c()
    build(colsg, 0, g1[...].astype(F32))
    step_c(1)
    step_b(2)
    slope = conv_flip(colsg, w1, 0, pixels)
    gfeat[...] = (
        gs[...].reshape(pixels, chan)
        + slope * silu_slope(fmap[pl.ds(edge, pixels)].astype(F32))
    ).astype(BF16)
    step_a(3)
    step_c(2)
    step_b(3)
    step_c(3)

    for way in range(2):
        halo_sent(0, feat, fmap, way)
        halo_sent(1, g2, g2, way)

    def store_a(u, value):
        attn_out[:, pl.ds(u * unit, unit), :] = value.astype(attn_out.dtype)

    def store_conv(i):
        def store(u, value):
            size = value.shape[0]
            conv_out[i, pl.ds(u * size, size), :] = value.astype(conv_out.dtype)

        return store

    finish_a(store_a)
    finish_b(store_conv(1))
    finish_c(store_conv(0))


def run_full(
    dims, feat, cot, w1h, w2h, wqh, wkh, wvh, woh, gfeat, conv_out, attn_out,
    w1, w2, wq, wk, wv, wo, load,
    fmap, cotv, cols1, cols2, colsg, hidden, normed, normed_f, inv, g2, gs, g1, acc,
    normp, cotp, backp, gn, gq, gk, gv, mx,
    part_a, part_b, part_c, r1a, r1b, r1c,
    t2a, t2b, t2c, r3a, r3b, r3c, r4a, r4b, r4c,
    near_send, near_recv, swap_send, swap_recv,
    cot_send, cot_recv, nrm_send, nrm_recv, bck_send, bck_recv,
    s1_send, s1_recv, s2_send, s2_recv, s3_send, s3_recv, s4_send, s4_recv,
):
    views, strips, rows, width, chan = dims
    pixels = rows * width
    half = pixels // CHUNKS
    block = rows // CHUNKS
    share = half // views
    every = strips * pixels
    lanes = chan // strips
    zs = views // 2
    view = lax.axis_index("view")
    strip = lax.axis_index("strip")
    core = lax.rem(view, 2)
    zed = lax.div(view, 2)
    other = 1 - strip
    mine = pl.ds(pl.multiple_of(view * share, share), share)
    columns = pl.ds(pl.multiple_of(strip * lanes, lanes), lanes)

    def span(row, count):
        return pl.ds(pl.multiple_of(row * width, width), count * width)

    barrier = pltpu.get_barrier_semaphore()
    for k in range(1, views):
        pl.semaphore_signal(
            barrier, inc=1, device_id={"view": lax.rem(view + k, views)}, device_id_type=MESH
        )
    pl.semaphore_signal(barrier, inc=1, device_id={"strip": other}, device_id_type=MESH)
    loads = [
        pltpu.make_async_copy(src, dst, load.at[i])
        for i, (src, dst) in enumerate(
            (
                (feat, fmap.at[span(strip * rows, rows)]),
                (w1h, w1), (w2h, w2), (woh, wo), (wqh, wq), (wkh, wk), (wvh, wv), (cot, cotv),
            )
        )
    ]
    for item in loads:
        item.start()
    for cols in (cols1, cols2, colsg):
        cols[pl.ds(0, width)] = jnp.zeros((width, 3 * chan), BF16)
        cols[pl.ds(width + every, width)] = jnp.zeros((width, 3 * chan), BF16)
    g1[pl.ds(0, width)] = jnp.zeros((width, chan), BF16)
    g1[pl.ds(width + every, width)] = jnp.zeros((width, chan), BF16)
    pl.semaphore_wait(barrier, views)

    def start(copies):
        for copy in copies:
            copy.start()

    def wait(copies):
        for copy in copies:
            copy.wait()

    def first(h, which):
        return which * (3 * block) if h == 0 else block * (1 + which)

    def near_copies(h):
        out = []
        row = first(h, strip)
        for i in range(SPLIT):
            size = half // SPLIT
            place = pl.ds(pl.multiple_of(row * width + i * size, size), size)
            inside = pl.ds(pl.multiple_of((row - strip * rows) * width + i * size, size), size)
            out.append(
                pltpu.make_async_remote_copy(
                    src_ref=feat.at[inside], dst_ref=fmap.at[place],
                    send_sem=near_send.at[h, i], recv_sem=near_recv.at[h, i],
                    device_id={"strip": other}, device_id_type=MESH,
                )
            )
        return out

    def swap_copies(h):
        out = []
        row = first(h, strip)
        for i in range(SPLIT):
            size = half // SPLIT
            place = pl.ds(pl.multiple_of(row * width + i * size, size), size)
            out.append(
                pltpu.make_async_remote_copy(
                    src_ref=g2.at[place], dst_ref=g2.at[place],
                    send_sem=swap_send.at[h, i], recv_sem=swap_recv.at[h, i],
                    device_id={"strip": other}, device_id_type=MESH,
                )
            )
        return out

    def spread(src, dst, send, recv):
        out = []
        for k in range(1, views):
            peer = lax.rem(view + k, views)
            out.append(
                pltpu.make_async_remote_copy(
                    src_ref=src(pl.ds(pl.multiple_of(peer * share, share), share)),
                    dst_ref=dst(mine),
                    send_sem=send(k), recv_sem=recv(k),
                    device_id={"view": peer}, device_id_type=MESH,
                )
            )
        return out

    def from_cot(h, s):
        place = first(h, strip) - strip * rows
        return pl.ds(pl.multiple_of(place * width + s.start, share), share)

    def cot_copies(h):
        return spread(
            lambda s: cot.at[from_cot(h, s)], lambda s: cotp.at[h, s],
            lambda k: cot_send.at[h, k], lambda k: cot_recv.at[h, k],
        )

    def nrm_copies(h):
        return spread(
            lambda s: normed.at[h, s], lambda s: normp.at[h, s],
            lambda k: nrm_send.at[h, k], lambda k: nrm_recv.at[h, k],
        )

    def bck_copies(h):
        return spread(
            lambda s: backp.at[h, s], lambda s: gn.at[h, s],
            lambda k: bck_send.at[h, k], lambda k: bck_recv.at[h, k],
        )

    def build(cols, row, x):
        count = x.shape[0]
        place = span(row, count // width)
        column = lax.rem(lax.broadcasted_iota(jnp.int32, (count, chan), 0), width)
        left = jnp.where(column == 0, 0.0, pltpu.roll(x, 1, 0))
        right = jnp.where(column == width - 1, 0.0, pltpu.roll(x, count - 1, 0))
        cols[place, pl.ds(0, chan)] = left.astype(BF16)
        cols[place, pl.ds(chan, chan)] = x.astype(BF16)
        cols[place, pl.ds(2 * chan, chan)] = right.astype(BF16)

    def conv(cols, w, row, count):
        total = None
        for r in range(3):
            term = dot(cols[span(row + r, count), :], w[r])
            total = term if total is None else total + term
        return total

    def conv_flip(cols, w, row, count):
        total = None
        for r in range(3):
            for s in range(3):
                term = dot_nt(
                    cols[span(row + r, count), pl.ds(s * chan, chan)],
                    w[2 - r, pl.ds((2 - s) * chan, chan), :],
                )
                total = term if total is None else total + term
        return total

    def scatter(r, value, out):
        pieces, _, _, _, unit, _ = out.shape
        per = 3 * chan // unit
        for m in range(per):
            v, p = divmod(r * per + m, pieces)
            out[p, v // 2, v % 2, 0] = value[m * unit : (m + 1) * unit].astype(BF16)

    sems = (s1_send, s1_recv, s2_send, s2_recv, s3_send, s3_recv, s4_send, s4_recv)
    place = (view, strip, core, zed, views, strips, zs)
    count_a = part_a.shape[0]
    count_b = part_b.shape[0]
    launch_a, step_a, finish_a = group(
        place, sems, start, wait, 0, part_a, r1a, None, None, t2a, r3a, r4a
    )
    launch_b, step_b, finish_b = group(
        place, sems, start, wait, count_a, part_b, r1b, None, None, t2b, r3b, r4b, True
    )
    launch_c, step_c, finish_c = group(
        place, sems, start, wait, count_a + count_b, part_c, r1c, None, None, t2c, r3c, r4c, True
    )

    start(cot_copies(0))
    start(near_copies(1))
    start(near_copies(0))

    def forward(row, count):
        out = conv(cols1, w1, row, count).astype(BF16)
        hidden[span(row, count)] = out
        build(cols2, row + 1, silu(out.astype(F32)).astype(BF16).astype(F32))

    def columns_of(row, count):
        build(cols1, row + 1, silu(fmap[span(row, count)].astype(F32)))

    def norm(h):
        row = first(h, strip)
        x = fmap[span(row, block)].astype(F32)
        summed = (x + conv(cols2, w2, row, block)).astype(BF16).astype(F32)
        centred = summed - jnp.mean(summed, axis=-1, keepdims=True)
        scale = lax.rsqrt(jnp.mean(centred * centred, axis=-1, keepdims=True) + 1e-05)
        inv[h] = jnp.broadcast_to(scale, (half, 128))
        nf = centred * scale
        normed_f[h] = nf
        normed[h] = nf.astype(BF16)
        start(nrm_copies(h))
        normp[h, mine] = normed[h, mine]

    loads[0].wait()
    columns_of(strip * rows, rows)
    loads[1].wait()
    forward((rows + 1) * strip, rows - 1)
    loads[2].wait()
    norm(0)
    start(cot_copies(1))
    mark("norm0")
    wait(near_copies(1))
    columns_of(first(1, other), block)
    forward(rows - 1, 2)
    norm(1)
    mark("norm1")
    wait(near_copies(0))
    columns_of(first(0, other), block)
    forward((rows + 1) * other, rows - 1)
    for item in loads[3:]:
        item.wait()
    mark("forward")

    ia = lax.rem(lax.broadcasted_iota(jnp.int32, (half, half), 0), share)
    ib = lax.rem(lax.broadcasted_iota(jnp.int32, (half, half), 1), share)
    same = ia == ib
    factor = chan ** (-0.5)

    def attend(h):
        rp = normp[h]
        query = dot(rp, wq[...]).astype(BF16)
        key = dot(rp, wk[...]).astype(BF16)
        value = dot(rp, wv[...]).astype(BF16)
        scores = jnp.where(same, dot_nt(query, key) * factor, -jnp.inf)
        expo = jnp.exp(scores - jnp.max(scores, axis=-1, keepdims=True))
        prob_f = expo / jnp.sum(expo, axis=-1, keepdims=True)
        prob = prob_f.astype(BF16)
        gm = dot_nt(cotp[h], wo[...]).astype(BF16)
        grad_prob = dot_nt(gm, value)
        inner = jnp.sum(prob_f * grad_prob, axis=-1, keepdims=True)
        grad_score = (prob_f * (grad_prob - inner) * factor).astype(BF16)
        grad_value = dot_tn(prob, gm).astype(BF16)
        grad_query = dot(grad_score, key).astype(BF16)
        grad_key = dot_tn(grad_score, query).astype(BF16)
        back = (
            dot_nt(grad_query, wq[...]) + dot_nt(grad_key, wk[...]) + dot_nt(grad_value, wv[...])
        )
        backp[h] = back.astype(BF16)
        start(bck_copies(h))
        gn[h, mine] = backp[h, mine]
        gq[h] = grad_query
        gk[h] = grad_key
        gv[h] = grad_value
        mx[h] = dot(prob, value).astype(BF16)

    for h in range(CHUNKS):
        wait(cot_copies(h))
        cotp[h, mine] = cotv[from_cot(h, mine)]
        wait(nrm_copies(h))
        attend(h)
        mark("attend%d" % h)
    parts = part_a.shape[3]
    unit = chan // (views * parts)
    for t, (lhs, rhs) in enumerate(((normp, gq), (normp, gk), (normp, gv), (mx, cotp))):
        term = dot_tn(
            lhs[...].reshape(pixels, chan), rhs[...].reshape(pixels, chan)
        ).astype(BF16)
        for u in range(views * parts):
            v, q = divmod(u, parts)
            part_a[0, v // 2, v % 2, q, t] = term[u * unit : (u + 1) * unit]
    launch_a()
    mark("launch_a")

    def backward(h):
        row = first(h, strip)
        gnf = gn[h].astype(F32)
        nf = normed_f[h]
        gsum = cotv[span(row - strip * rows, block)].astype(F32) + inv[h, :, 0:1] * (
            gnf
            - jnp.mean(gnf, axis=-1, keepdims=True)
            - nf * jnp.mean(gnf * nf, axis=-1, keepdims=True)
        )
        gs[span(row - strip * rows, block)] = gsum
        g2[span(row, block)] = gsum.astype(BF16)
        start(swap_copies(h))
        build(colsg, row + 1, g2[span(row, block)].astype(F32))

    wait(bck_copies(0))
    backward(0)
    wait(bck_copies(1))
    backward(1)
    step_a(1)
    mark("backward")
    for r in range(3):
        acc[r] = dot_tn(
            cols2[span(strip * rows + r, rows)], g2[span(strip * rows, rows), columns]
        )
    for h in range(CHUNKS):
        wait(swap_copies(h))
        row = first(h, other)
        build(colsg, row + 1, g2[span(row, block)].astype(F32))
    mark("swapped")
    for r in range(3):
        term = dot_tn(cols2[span(other * rows + r, rows)], g2[span(other * rows, rows), columns])
        scatter(r, acc[r] + term, part_b)
    launch_b()
    mark("launch_b")

    def flipped(row):
        slope = conv_flip(colsg, w2, row, rows)
        own = slope * silu_slope(hidden[span(row, rows)].astype(F32))
        g1[span(row + 1, rows)] = own.astype(BF16)

    flipped(0)
    step_b(1)
    flipped(rows)
    for r in range(3):
        scatter(r, dot_tn(cols1[pl.ds(r * width, every)], g1[pl.ds(width, every), columns]), part_c)
    launch_c()
    mark("launch_c")
    build(colsg, 0, g1[span(strip * rows, rows + 2)].astype(F32))
    step_c(1)
    step_a(2)
    slope = conv_flip(colsg, w1, 0, rows)
    gfeat[...] = (
        gs[...] + slope * silu_slope(fmap[span(strip * rows, rows)].astype(F32))
    ).astype(BF16)
    mark("gfeat")
    step_b(2)
    mark("step_b2")
    step_c(2)
    mark("step_c2")

    def store_a(u, value):
        attn_out[:, pl.ds(u * unit, unit), :] = value.astype(attn_out.dtype)

    def store_conv(i):
        def store(u, value):
            p, t = divmod(u, strips)
            size = value.shape[0]
            conv_out[i, pl.ds(p * size, size), pl.ds(t * lanes, lanes)] = value.astype(
                conv_out.dtype
            )

        return store

    finish_a(store_a)
    finish_b(store_conv(1))
    finish_c(store_conv(0))


def widen(a, b, c, x, y, z):
    x[...] = a[...]
    y[...] = b[...].astype(F32)
    z[...] = c[...].astype(F32)


def body(features, cotangent, conv_first, conv_second, w_query, w_key, w_value, w_out):
    views = lax.axis_size("view")
    strips = lax.axis_size("strip")
    _, rows, width, chan = features.shape
    pixels = rows * width
    zs = views // 2
    cut = 9 * chan // views
    slab = chan // views
    vm = pltpu.VMEM
    dma = pltpu.SemaphoreType.DMA
    flat = (pixels, chan)
    split = (CHUNKS, pixels // CHUNKS, chan)
    wide = (rows + 2 * DEEP) * width
    near = (rows + 2) * width
    exact = cut % (16 * strips) == 0 and slab % (16 * strips) == 0
    parts = strips if exact else 1
    pieces = 3 if cut % (48 * parts) == 0 else 1
    full = strips == 2 and exact and pieces == 3 and rows == 2 * DEEP and chan % 256 == 0
    conv_u = (cut // (parts * pieces), chan)
    attn_u = (4, slab // parts, chan)
    units = ((1, attn_u), (pieces, conv_u), (pieces, conv_u))
    total = 1 + 2 * pieces
    hold = {
        "part_": [(n, zs, 2, parts) + u for n, u in units],
        "r1": [(n, zs, parts) + u for n, u in units],
        "t1": [(n, parts, zs) + u for n, u in units],
        "r2": [(n, max(parts - 1, 1), zs) + u for n, u in units],
        "t2": [(n, zs) + u for n, u in units],
        "r3": [(n, zs - 1) + u for n, u in units],
        "r4": [(n, strips) + u for n, u in units],
    }
    conv_k = (3, 3 * chan, chan)
    square = (chan, chan)
    scratch = {
        "w1": vm(conv_k, BF16), "w2": vm(conv_k, BF16),
        "wq": vm(square, BF16), "wk": vm(square, BF16),
        "wv": vm(square, BF16), "wo": vm(square, BF16), "load": dma((9,)),
        "fmap": vm((wide, chan), BF16), "cotv": vm(split, BF16),
        "cols1": vm((wide, 3 * chan), BF16), "cols2": vm((near, 3 * chan), BF16),
        "colsg": vm((wide, 3 * chan), BF16),
        "hidden": vm((near, chan), BF16), "normed": vm(split, BF16), "normed_f": vm(split, F32),
        "inv": vm(split[:2] + (128,), F32), "g2": vm((wide, chan), BF16), "gs": vm(split, F32),
        "g1": vm((near, chan), BF16),
    }
    for name in ("normp", "cotp", "backp", "gn", "gq", "gk", "gv", "mx"):
        scratch[name] = vm(split, BF16)
    for name, shapes in hold.items():
        for letter, shape in zip("abc", shapes):
            scratch[name + letter] = vm(shape, BF16)
    if full:
        conv_u = (cut // pieces, chan // strips)
        attn_u = (4, slab, chan)
        scratch["part_a"] = vm((1, zs, 2, 1) + attn_u, BF16)
        scratch["r1a"] = vm((1, zs, 1) + attn_u, BF16)
        scratch["t2a"] = vm((1, zs) + attn_u, BF16)
        scratch["r3a"] = vm((1, zs - 1) + attn_u, BF16)
        scratch["r4a"] = vm((1, strips) + attn_u, BF16)
        del scratch["t1a"], scratch["r2a"]
        for letter in "bc":
            scratch["part_" + letter] = vm((pieces, zs, 2, 1) + conv_u, BF16)
            scratch["r1" + letter] = vm((pieces, zs, 1) + conv_u, BF16)
            scratch["t2" + letter] = vm((pieces, zs) + conv_u, BF16)
            scratch["r3" + letter] = vm((pieces, zs - 1) + conv_u, BF16)
            scratch["r4" + letter] = vm((pieces, strips) + conv_u, BF16)
            del scratch["t1" + letter], scratch["r2" + letter]
        padded = (strips * rows + 2) * width
        for name in ("cols1", "cols2", "colsg"):
            scratch[name] = vm((padded, 3 * chan), BF16)
        for name in ("fmap", "hidden", "g2"):
            scratch[name] = vm((strips * pixels, chan), BF16)
        scratch["g1"] = vm((padded, chan), BF16)
        scratch["cotv"] = vm(flat, BF16)
        scratch["gs"] = vm(flat, F32)
        scratch["acc"] = vm((3, 3 * chan, chan // strips), F32)
    counts = {
        "halo": (2, 2), "cot": (views,), "nrm": (CHUNKS, views), "bck": (CHUNKS, views),
        "s1": (total,), "s2": (total, strips), "s3": (total, zs), "s4": (total, strips),
    }
    if full:
        del counts["halo"]
        counts["near"] = counts["swap"] = (CHUNKS, SPLIT)
        counts["cot"] = (CHUNKS, views)
    for name, shape in counts.items():
        scratch[name + "_send"] = dma(shape)
        scratch[name + "_recv"] = dma(shape)
    names = (
        "feat", "cot", "w1h", "w2h", "wqh", "wkh", "wvh", "woh", "gfeat", "conv_out", "attn_out",
    ) + tuple(scratch)
    spec = pl.BlockSpec(memory_space=pltpu.VMEM)
    stay = pl.BlockSpec(memory_space=pl.ANY)
    kind = BF16 if exact else F32
    conv_s = (2, cut, chan)
    attn_s = (4, slab, chan)
    outs = pl.pallas_call(
        functools.partial(
            kernel, run_full if full else run, (views, strips, rows, width, chan), names
        ),
        out_shape=(
            jax.ShapeDtypeStruct(flat, BF16),
            jax.ShapeDtypeStruct(conv_s, kind),
            jax.ShapeDtypeStruct(attn_s, kind),
        ),
        in_specs=[stay] * 8,
        out_specs=(spec, spec, spec),
        scratch_shapes=list(scratch.values()),
        compiler_params=pltpu.CompilerParams(
            collective_id=0, has_side_effects=True, vmem_limit_bytes=48 * 1024 * 1024
        ),
    )(
        *[
            pltpu.with_memory_space_constraint(x, pltpu.HBM)
            for x in (
                features.reshape(flat),
                cotangent.reshape(flat if full else split),
                conv_first.reshape(3, 3 * chan, chan),
                conv_second.reshape(3, 3 * chan, chan),
                w_query, w_key, w_value, w_out,
            )
        ]
    )
    outs = pl.pallas_call(
        widen,
        out_shape=(
            jax.ShapeDtypeStruct(flat, BF16),
            jax.ShapeDtypeStruct(conv_s, F32),
            jax.ShapeDtypeStruct(attn_s, F32),
        ),
        in_specs=[spec] * 3,
        out_specs=(spec, spec, spec),
        compiler_params=pltpu.CompilerParams(vmem_limit_bytes=8 * 1024 * 1024),
    )(*outs)
    return (outs[0].reshape(features.shape), outs[1], outs[2])


def solution(mesh):
    rows = P(("orbit", "view"), "strip", None, None)
    grads = P("orbit", "view", None)
    return jax.shard_map(
        body,
        mesh=mesh,
        in_specs=(rows, rows, P(), P(), P(), P(), P(), P()),
        out_specs=(rows, grads, grads),
        check_vma=False,
    )
```

```python
import functools

import jax
import jax.numpy as jnp
from jax import lax
from jax.experimental import pallas as pl
from jax.experimental.pallas import tpu as pltpu
from jax.sharding import PartitionSpec as P

MESH = pl.DeviceIdType.MESH
F32 = jnp.float32
BF16 = jnp.bfloat16
NT = (((1,), (1,)), ((), ()))
TN = (((0,), (0,)), ((), ()))
CHUNKS = 2
DEEP = 2
SPLIT = 1
PARCELS = 4


def dot(a, b):
    return jnp.dot(a, b, preferred_element_type=F32)


def dot_nt(a, b):
    return lax.dot_general(a, b, NT, preferred_element_type=F32)


def dot_tn(a, b):
    return lax.dot_general(a, b, TN, preferred_element_type=F32)


def silu(x):
    return x * jax.nn.sigmoid(x)


def silu_slope(x):
    sigma = jax.nn.sigmoid(x)
    return sigma * (1.0 + x * (1.0 - sigma))


def group(place, sems, start, wait, base, part, r1, t1, r2, t2, r3, r4, split=False):
    view, strip, core, zed, views, strips, zs = place
    s1_send, s1_recv, s2_send, s2_recv, s3_send, s3_recv, s4_send, s4_recv = sems
    parts = part.shape[3]
    shares = split or parts > 1

    def stage1(p):
        return [
            pltpu.make_async_remote_copy(
                src_ref=part.at[p, :, 1 - core], dst_ref=r1.at[p],
                send_sem=s1_send.at[base + p], recv_sem=s1_recv.at[base + p],
                device_id={"view": view + 1 - 2 * core}, device_id_type=MESH,
            )
        ]

    def reduce1(p):
        for j in range(zs):
            if t1 is None:
                t2[p, j] = (
                    part[p, j, core, 0].astype(F32) + r1[p, j, 0].astype(F32)
                ).astype(BF16)
                continue
            for t in range(parts):
                t1[p, t, j] = (
                    part[p, j, core, t].astype(F32) + r1[p, j, t].astype(F32)
                ).astype(BF16)

    def stage2(p):
        out = []
        for k in range(1, parts):
            other = lax.rem(strip + k, strips)
            out.append(
                pltpu.make_async_remote_copy(
                    src_ref=t1.at[p, other], dst_ref=r2.at[p, k - 1],
                    send_sem=s2_send.at[base + p, k], recv_sem=s2_recv.at[base + p, k],
                    device_id={"strip": other}, device_id_type=MESH,
                )
            )
        return out

    def reduce2(p):
        own = strip if parts > 1 else 0
        for j in range(zs):
            value = t1[p, own, j].astype(F32)
            for k in range(1, parts):
                value = value + r2[p, k - 1, j].astype(F32)
            t2[p, j] = value.astype(BF16)

    def stage3(p):
        out = []
        for k in range(1, zs):
            other = lax.rem(zed + k, zs)
            out.append(
                pltpu.make_async_remote_copy(
                    src_ref=t2.at[p, other], dst_ref=r3.at[p, k - 1],
                    send_sem=s3_send.at[base + p, k], recv_sem=s3_recv.at[base + p, k],
                    device_id={"view": other * 2 + core}, device_id_type=MESH,
                )
            )
        return out

    def reduce3(p):
        value = t2[p, zed].astype(F32)
        for k in range(1, zs):
            value = value + r3[p, k - 1].astype(F32)
        r4[p, strip] = value.astype(BF16)

    def stage4(p):
        out = []
        for k in range(1, strips):
            out.append(
                pltpu.make_async_remote_copy(
                    src_ref=r4.at[p, strip], dst_ref=r4.at[p, strip],
                    send_sem=s4_send.at[base + p, k], recv_sem=s4_recv.at[base + p, k],
                    device_id={"strip": lax.rem(strip + k, strips)}, device_id_type=MESH,
                )
            )
        return out

    def final(p):
        if shares:
            return [r4[p, t].astype(F32) for t in range(strips)]
        value = r4[p, 0].astype(F32)
        for t in range(1, strips):
            value = value + r4[p, t].astype(F32)
        return [value]

    reduces = (None, reduce1, reduce2, reduce3)
    stages = (stage1, stage2, stage3, stage4)
    if t1 is None:
        reduces = (None, reduce1, reduce3)
        stages = (stage1, stage3, stage4)

    def launch():
        for p in range(part.shape[0]):
            start(stage1(p))

    def advance(k, p):
        wait(stages[k - 1](p))
        reduces[k](p)
        start(stages[k](p))

    def advance_all(k):
        for p in range(part.shape[0]):
            advance(k, p)

    def finish(store):
        for p in range(part.shape[0]):
            wait(stage4(p))
            for t, value in enumerate(final(p)):
                store(p * (strips if shares else 1) + t, value)

    return launch, advance_all, finish


def mark(name):
    pass


def kernel(call, dims, names, *refs):
    call(dims, **dict(zip(names, refs, strict=True)))


def run(
    dims, feat, cot, w1h, w2h, wqh, wkh, wvh, woh, gfeat, conv_out, attn_out,
    w1, w2, wq, wk, wv, wo, load,
    fmap, cotv, cols1, cols2, colsg, hidden, normed, normed_f, inv, g2, gs, g1,
    normp, cotp, backp, gn, gq, gk, gv, mx,
    part_a, part_b, part_c, r1a, r1b, r1c, t1a, t1b, t1c, r2a, r2b, r2c,
    t2a, t2b, t2c, r3a, r3b, r3c, r4a, r4b, r4c,
    halo_send, halo_recv, cot_send, cot_recv, nrm_send, nrm_recv, bck_send, bck_recv,
    s1_send, s1_recv, s2_send, s2_recv, s3_send, s3_recv, s4_send, s4_recv,
):
    views, strips, rows, width, chan = dims
    pixels = rows * width
    half = pixels // CHUNKS
    share = half // views
    edge = DEEP * width
    zs = views // 2
    view = lax.axis_index("view")
    strip = lax.axis_index("strip")
    core = lax.rem(view, 2)
    zed = lax.div(view, 2)

    barrier = pltpu.get_barrier_semaphore()
    for k in range(1, views):
        pl.semaphore_signal(
            barrier, inc=1, device_id={"view": lax.rem(view + k, views)}, device_id_type=MESH
        )
    for k in range(1, strips):
        pl.semaphore_signal(
            barrier, inc=1, device_id={"strip": lax.rem(strip + k, strips)}, device_id_type=MESH
        )
    mine = pl.ds(pl.multiple_of(view * share, share), share)
    loads = [
        pltpu.make_async_copy(src, dst, load.at[i])
        for i, (src, dst) in enumerate(
            (
                (feat, fmap.at[pl.ds(edge, pixels)]),
                (w1h, w1), (w2h, w2), (woh, wo), (wqh, wq), (wkh, wk), (wvh, wv),
                (cot.at[:, mine], cotp.at[:, mine]), (cot, cotv),
            )
        )
    ]
    for item in loads:
        item.start()

    @pl.when(strip == 0)
    def _():
        fmap[pl.ds(0, edge)] = jnp.zeros((edge, chan), BF16)
        g2[pl.ds(0, edge)] = jnp.zeros((edge, chan), BF16)

    @pl.when(strip == strips - 1)
    def _():
        fmap[pl.ds(edge + pixels, edge)] = jnp.zeros((edge, chan), BF16)
        g2[pl.ds(edge + pixels, edge)] = jnp.zeros((edge, chan), BF16)

    pl.semaphore_wait(barrier, views - 1 + strips - 1)

    def halo_copy(e, src, dst, way):
        start = 0 if way == 0 else pixels - edge
        land = edge + pixels if way == 0 else 0
        near = lax.max(strip - 1, 0) if way == 0 else lax.min(strip + 1, strips - 1)
        base = edge if src is dst else 0
        return pltpu.make_async_remote_copy(
            src_ref=src.at[pl.ds(base + start, edge)], dst_ref=dst.at[pl.ds(land, edge)],
            send_sem=halo_send.at[e, way], recv_sem=halo_recv.at[e, way],
            device_id={"strip": near}, device_id_type=MESH,
        )

    def halo_start(e, src, dst, way):
        copy = halo_copy(e, src, dst, way)
        pl.when(strip > 0 if way == 0 else strip < strips - 1)(copy.start)

    def halo_sent(e, src, dst, way):
        copy = halo_copy(e, src, dst, way)
        pl.when(strip > 0 if way == 0 else strip < strips - 1)(copy.wait_send)

    def halo_here(e, src, dst, way):
        copy = halo_copy(e, src, dst, way)
        pl.when(strip < strips - 1 if way == 0 else strip > 0)(copy.wait_recv)

    def spread(src, dst, send, recv):
        out = []
        for k in range(1, views):
            peer = lax.rem(view + k, views)
            out.append(
                pltpu.make_async_remote_copy(
                    src_ref=src(pl.ds(pl.multiple_of(peer * share, share), share)),
                    dst_ref=dst(mine),
                    send_sem=send(k), recv_sem=recv(k),
                    device_id={"view": peer}, device_id_type=MESH,
                )
            )
        return out

    def start(copies):
        for copy in copies:
            copy.start()

    def wait(copies):
        for copy in copies:
            copy.wait()

    def build(cols, offset, x):
        count = x.shape[0]
        column = lax.rem(lax.broadcasted_iota(jnp.int32, (count, chan), 0), width)
        left = jnp.where(column == 0, 0.0, pltpu.roll(x, 1, 0))
        right = jnp.where(column == width - 1, 0.0, pltpu.roll(x, count - 1, 0))
        cols[pl.ds(offset, count), pl.ds(0, chan)] = left.astype(BF16)
        cols[pl.ds(offset, count), pl.ds(chan, chan)] = x.astype(BF16)
        cols[pl.ds(offset, count), pl.ds(2 * chan, chan)] = right.astype(BF16)

    def conv(cols, w, offset, count):
        total = None
        for r in range(3):
            term = dot(cols[pl.ds(offset + r * width, count), :], w[r])
            total = term if total is None else total + term
        return total

    def conv_flip(cols, w, offset, count):
        total = None
        for r in range(3):
            for s in range(3):
                term = dot_nt(
                    cols[pl.ds(offset + r * width, count), pl.ds(s * chan, chan)],
                    w[2 - r, pl.ds((2 - s) * chan, chan), :],
                )
                total = term if total is None else total + term
        return total

    def wgrad(cols, offset, d, out):
        pieces, _, _, parts, unit, _ = out.shape
        per = 3 * chan // unit
        for r in range(3):
            value = dot_tn(cols[pl.ds(offset + r * width, pixels), :], d).astype(BF16)
            for m in range(per):
                u = r * per + m
                v, rest = divmod(u, pieces * parts)
                p, t = divmod(rest, parts)
                out[p, v // 2, v % 2, t] = value[m * unit : (m + 1) * unit]

    def inside(x, first, last):
        if first:
            low = lax.broadcasted_iota(jnp.int32, x.shape, 0)
            x = jnp.where(jnp.logical_and(low < width, strip == 0), 0.0, x)
        if last:
            high = lax.broadcasted_iota(jnp.int32, x.shape, 0)
            gone = jnp.logical_and(high >= x.shape[0] - width, strip == strips - 1)
            x = jnp.where(gone, 0.0, x)
        return x

    sems = (s1_send, s1_recv, s2_send, s2_recv, s3_send, s3_recv, s4_send, s4_recv)
    place = (view, strip, core, zed, views, strips, zs)
    count_a = part_a.shape[0]
    count_b = part_b.shape[0]
    launch_a, step_a, finish_a = group(
        place, sems, start, wait, 0, part_a, r1a, t1a, r2a, t2a, r3a, r4a
    )
    launch_b, step_b, finish_b = group(
        place, sems, start, wait, count_a, part_b, r1b, t1b, r2b, t2b, r3b, r4b
    )
    launch_c, step_c, finish_c = group(
        place, sems, start, wait, count_a + count_b, part_c, r1c, t1c, r2c, t2c, r3c, r4c
    )

    halo_start(0, feat, fmap, 0)
    halo_start(0, feat, fmap, 1)
    cot_copies = spread(
        lambda s: cot.at[:, s], lambda s: cotp.at[:, s],
        lambda k: cot_send.at[k], lambda k: cot_recv.at[k],
    )
    start(cot_copies)

    def forward(row, count, first=False, last=False):
        out = conv(cols1, w1, row * width, count * width).astype(BF16)
        hidden[pl.ds(row * width, count * width)] = out
        act = silu(out.astype(F32)).astype(BF16).astype(F32)
        build(cols2, row * width, inside(act, first, last))

    def nrm_copies(h):
        return spread(
            lambda s: normed.at[h, s], lambda s: normp.at[h, s],
            lambda k: nrm_send.at[h, k], lambda k: nrm_recv.at[h, k],
        )

    def norm(h):
        offset = h * half
        x = fmap[pl.ds(edge + offset, half)].astype(F32)
        summed = (x + conv(cols2, w2, offset, half)).astype(BF16).astype(F32)
        centred = summed - jnp.mean(summed, axis=-1, keepdims=True)
        scale = lax.rsqrt(jnp.mean(centred * centred, axis=-1, keepdims=True) + 1e-05)
        inv[h] = jnp.broadcast_to(scale, (half, 128))
        nf = centred * scale
        normed_f[h] = nf
        normed[h] = nf.astype(BF16)
        start(nrm_copies(h))
        normp[h, mine] = normed[h, mine]

    loads[0].wait()
    build(cols1, edge, silu(fmap[pl.ds(edge, pixels)].astype(F32)))
    loads[1].wait()
    forward(DEEP, rows - DEEP)
    halo_here(0, feat, fmap, 1)
    build(cols1, 0, silu(fmap[pl.ds(0, edge)].astype(F32)))
    forward(0, DEEP, first=True)
    loads[2].wait()
    norm(0)
    halo_here(0, feat, fmap, 0)
    build(cols1, edge + pixels, silu(fmap[pl.ds(edge + pixels, edge)].astype(F32)))
    forward(rows, DEEP, last=True)
    norm(1)
    mark("normed")

    for item in loads[3:]:
        item.wait()
    wait(cot_copies)
    gmix = dot_nt(cotp[...].reshape(pixels, chan), wo[...]).astype(BF16)
    ia = lax.rem(lax.broadcasted_iota(jnp.int32, (half, half), 0), share)
    ib = lax.rem(lax.broadcasted_iota(jnp.int32, (half, half), 1), share)
    same = ia == ib
    factor = chan ** (-0.5)

    def bck_copies(h):
        return spread(
            lambda s: backp.at[h, s], lambda s: gn.at[h, s],
            lambda k: bck_send.at[h, k], lambda k: bck_recv.at[h, k],
        )

    def attend(h):
        rp = normp[h]
        gm = gmix[h * half : (h + 1) * half]
        query = dot(rp, wq[...]).astype(BF16)
        key = dot(rp, wk[...]).astype(BF16)
        value = dot(rp, wv[...]).astype(BF16)
        scores = jnp.where(same, dot_nt(query, key) * factor, -jnp.inf)
        expo = jnp.exp(scores - jnp.max(scores, axis=-1, keepdims=True))
        prob_f = expo / jnp.sum(expo, axis=-1, keepdims=True)
        prob = prob_f.astype(BF16)
        grad_prob = dot_nt(gm, value)
        inner = jnp.sum(prob_f * grad_prob, axis=-1, keepdims=True)
        grad_score = (prob_f * (grad_prob - inner) * factor).astype(BF16)
        grad_value = dot_tn(prob, gm).astype(BF16)
        grad_query = dot(grad_score, key).astype(BF16)
        grad_key = dot_tn(grad_score, query).astype(BF16)
        back = (
            dot_nt(grad_query, wq[...]) + dot_nt(grad_key, wk[...]) + dot_nt(grad_value, wv[...])
        )
        backp[h] = back.astype(BF16)
        start(bck_copies(h))
        gn[h, mine] = backp[h, mine]
        gq[h] = grad_query
        gk[h] = grad_key
        gv[h] = grad_value
        mx[h] = dot(prob, value).astype(BF16)

    for h in range(CHUNKS):
        wait(nrm_copies(h))
        attend(h)
    mark("attended")
    parts = part_a.shape[3]
    unit = chan // (views * parts)
    for t, (lhs, rhs) in enumerate(((normp, gq), (normp, gk), (normp, gv), (mx, cotp))):
        term = dot_tn(
            lhs[...].reshape(pixels, chan), rhs[...].reshape(pixels, chan)
        ).astype(BF16)
        for u in range(views * parts):
            v, q = divmod(u, parts)
            part_a[0, v // 2, v % 2, q, t] = term[u * unit : (u + 1) * unit]
    launch_a()

    def backward(h):
        gnf = gn[h].astype(F32)
        nf = normed_f[h]
        gsum = cotv[h].astype(F32) + inv[h, :, 0:1] * (
            gnf
            - jnp.mean(gnf, axis=-1, keepdims=True)
            - nf * jnp.mean(gnf * nf, axis=-1, keepdims=True)
        )
        gs[h] = gsum
        g2[pl.ds(edge + h * half, half)] = gsum.astype(BF16)

    step_a(1)
    for h in range(CHUNKS):
        wait(bck_copies(h))
        backward(h)
        if h == 0:
            halo_start(1, g2, g2, 0)
    halo_start(1, g2, g2, 1)
    mark("g2")
    wgrad(cols2, 0, g2[pl.ds(edge, pixels)], part_b)
    launch_b()
    build(colsg, edge, g2[pl.ds(edge, pixels)].astype(F32))
    step_a(2)
    step_b(1)

    def flipped(row, count, first=False, last=False):
        slope = conv_flip(colsg, w2, row * width, count * width)
        own = slope * silu_slope(hidden[pl.ds(row * width, count * width)].astype(F32))
        g1[pl.ds(row * width, count * width)] = inside(own, first, last).astype(BF16)

    halo_here(1, g2, g2, 1)
    build(colsg, 0, g2[pl.ds(0, edge)].astype(F32))
    halo_here(1, g2, g2, 0)
    build(colsg, edge + pixels, g2[pl.ds(edge + pixels, edge)].astype(F32))
    flipped(0, rows + 2, True, True)
    mark("g1")
    wgrad(cols1, width, g1[pl.ds(width, pixels)], part_c)
    launch_c()
    build(colsg, 0, g1[...].astype(F32))
    step_c(1)
    step_b(2)
    slope = conv_flip(colsg, w1, 0, pixels)
    gfeat[...] = (
        gs[...].reshape(pixels, chan)
        + slope * silu_slope(fmap[pl.ds(edge, pixels)].astype(F32))
    ).astype(BF16)
    step_a(3)
    step_c(2)
    step_b(3)
    step_c(3)

    for way in range(2):
        halo_sent(0, feat, fmap, way)
        halo_sent(1, g2, g2, way)

    def store_a(u, value):
        attn_out[:, pl.ds(u * unit, unit), :] = value.astype(attn_out.dtype)

    def store_conv(i):
        def store(u, value):
            size = value.shape[0]
            conv_out[i, pl.ds(u * size, size), :] = value.astype(conv_out.dtype)

        return store

    finish_a(store_a)
    finish_b(store_conv(1))
    finish_c(store_conv(0))


def run_full(
    dims, feat, cot, w1h, w2h, wqh, wkh, wvh, woh, gfeat, conv_out, attn_out,
    w1, w2, wq, wk, wv, wo, load,
    fmap, cotv, cols1, cols2, colsg, hidden, normed, normed_f, inv, g2, gs, g1, acc, acc1, w2t, slope2,
    normp, cotp, backp, gn, gq, gk, gv, mx,
    part_a, part_b, part_c, r1a, r1b, r1c,
    t2a, t2b, t2c, r3a, r3b, r3c, r4a, r4b, r4c,
    near_send, near_recv, swap_send, swap_recv,
    cot_send, cot_recv, nrm_send, nrm_recv, bck_send, bck_recv,
    s1_send, s1_recv, s2_send, s2_recv, s3_send, s3_recv, s4_send, s4_recv,
):
    views, strips, rows, width, chan = dims
    pixels = rows * width
    chunks = normp.shape[0]
    piece = pixels // chunks
    block = rows // 2
    each = rows // chunks
    per = chunks // 2
    share = piece // views
    every = strips * pixels
    lanes = chan // strips
    zs = views // 2
    view = lax.axis_index("view")
    strip = lax.axis_index("strip")
    core = lax.rem(view, 2)
    zed = lax.div(view, 2)
    other = 1 - strip
    mine = pl.ds(pl.multiple_of(view * share, share), share)
    columns = pl.ds(pl.multiple_of(strip * lanes, lanes), lanes)

    def span(row, count):
        return pl.ds(pl.multiple_of(row * width, width), count * width)

    barrier = pltpu.get_barrier_semaphore()
    for k in range(1, views):
        pl.semaphore_signal(
            barrier, inc=1, device_id={"view": lax.rem(view + k, views)}, device_id_type=MESH
        )
    pl.semaphore_signal(barrier, inc=1, device_id={"strip": other}, device_id_type=MESH)
    loads = [
        pltpu.make_async_copy(src, dst, load.at[i])
        for i, (src, dst) in enumerate(
            (
                (feat, fmap.at[span(strip * rows, rows)]),
                (w1h, w1), (w2h, w2), (woh, wo), (wqh, wq), (wkh, wk), (wvh, wv), (cot, cotv),
            )
        )
    ]
    for item in loads:
        item.start()
    for cols in (cols1, cols2, colsg):
        cols[pl.ds(0, width)] = jnp.zeros((width, 3 * chan), BF16)
        cols[pl.ds(width + every, width)] = jnp.zeros((width, 3 * chan), BF16)
    g1[pl.ds(0, width)] = jnp.zeros((width, chan), BF16)
    g1[pl.ds(width + every, width)] = jnp.zeros((width, chan), BF16)
    pl.semaphore_wait(barrier, views)

    def start(copies):
        for copy in copies:
            copy.start()

    def wait(copies):
        for copy in copies:
            copy.wait()

    def first(k, which):
        return which * (3 * block) if k == 0 else block * (1 + which)

    def start_row(h, which):
        return first(h // per, which) + (h % per) * each

    def near_copies(k):
        out = []
        row = first(k, strip)
        for i in range(SPLIT):
            size = block * width // SPLIT
            place = pl.ds(pl.multiple_of(row * width + i * size, size), size)
            inside = pl.ds(pl.multiple_of((row - strip * rows) * width + i * size, size), size)
            out.append(
                pltpu.make_async_remote_copy(
                    src_ref=feat.at[inside], dst_ref=fmap.at[place],
                    send_sem=near_send.at[k, i], recv_sem=near_recv.at[k, i],
                    device_id={"strip": other}, device_id_type=MESH,
                )
            )
        return out

    def swap_copies(h, part):
        place = span(start_row(h, strip), each)
        which = pl.ds(pl.multiple_of((strip if part else other) * lanes, lanes), lanes)
        return [
            pltpu.make_async_remote_copy(
                src_ref=g2.at[place, which], dst_ref=g2.at[place, which],
                send_sem=swap_send.at[h, part], recv_sem=swap_recv.at[h, part],
                device_id={"strip": other}, device_id_type=MESH,
            )
        ]

    def spread(src, dst, send, recv):
        out = []
        for k in range(1, views):
            peer = lax.rem(view + k, views)
            out.append(
                pltpu.make_async_remote_copy(
                    src_ref=src(pl.ds(pl.multiple_of(peer * share, share), share)),
                    dst_ref=dst(mine),
                    send_sem=send(k), recv_sem=recv(k),
                    device_id={"view": peer}, device_id_type=MESH,
                )
            )
        return out

    def from_cot(h, s):
        place = start_row(h, strip) - strip * rows
        return pl.ds(pl.multiple_of(place * width + s.start, share), share)

    def cot_copies(h):
        return spread(
            lambda s: cot.at[from_cot(h, s)], lambda s: cotp.at[h, s],
            lambda k: cot_send.at[h, k], lambda k: cot_recv.at[h, k],
        )

    def nrm_copies(h):
        return spread(
            lambda s: normed.at[h, s], lambda s: normp.at[h, s],
            lambda k: nrm_send.at[h, k], lambda k: nrm_recv.at[h, k],
        )

    def bck_copies(h):
        return spread(
            lambda s: backp.at[h, s], lambda s: gn.at[h, s],
            lambda k: bck_send.at[h, k], lambda k: bck_recv.at[h, k],
        )

    def build(cols, row, x):
        count = x.shape[0]
        place = span(row, count // width)
        column = lax.rem(lax.broadcasted_iota(jnp.int32, (count, chan), 0), width)
        left = jnp.where(column == 0, 0.0, pltpu.roll(x, 1, 0))
        right = jnp.where(column == width - 1, 0.0, pltpu.roll(x, count - 1, 0))
        cols[place, pl.ds(0, chan)] = left.astype(BF16)
        cols[place, pl.ds(chan, chan)] = x.astype(BF16)
        cols[place, pl.ds(2 * chan, chan)] = right.astype(BF16)

    def conv(cols, w, row, count):
        total = None
        for r in range(3):
            term = dot(cols[span(row + r, count), :], w[r])
            total = term if total is None else total + term
        return total

    def conv_flip(cols, w, row, count):
        total = None
        for r in range(3):
            for s in range(3):
                term = dot_nt(
                    cols[span(row + r, count), pl.ds(s * chan, chan)],
                    w[2 - r, pl.ds((2 - s) * chan, chan), :],
                )
                total = term if total is None else total + term
        return total

    def scatter(r, value, out):
        pieces, _, _, _, unit, _ = out.shape
        per = 3 * chan // unit
        for m in range(per):
            v, p = divmod(r * per + m, pieces)
            out[p, v // 2, v % 2, 0] = value[m * unit : (m + 1) * unit].astype(BF16)

    sems = (s1_send, s1_recv, s2_send, s2_recv, s3_send, s3_recv, s4_send, s4_recv)
    place = (view, strip, core, zed, views, strips, zs)
    count_a = part_a.shape[0]
    count_b = part_b.shape[0]
    launch_a, step_a, finish_a = group(
        place, sems, start, wait, 0, part_a, r1a, None, None, t2a, r3a, r4a
    )
    launch_b, step_b, finish_b = group(
        place, sems, start, wait, count_a, part_b, r1b, None, None, t2b, r3b, r4b, True
    )
    launch_c, step_c, finish_c = group(
        place, sems, start, wait, count_a + count_b, part_c, r1c, None, None, t2c, r3c, r4c, True
    )

    for h in range(per):
        start(cot_copies(h))
    start(near_copies(1))
    start(near_copies(0))

    def forward(row, count):
        out = conv(cols1, w1, row, count).astype(BF16)
        hidden[span(row, count)] = out
        build(cols2, row + 1, silu(out.astype(F32)).astype(BF16).astype(F32))

    def columns_of(row, count):
        build(cols1, row + 1, silu(fmap[span(row, count)].astype(F32)))

    def norm(k):
        row = first(k, strip)
        x = fmap[span(row, block)].astype(F32)
        summed = (x + conv(cols2, w2, row, block)).astype(BF16).astype(F32)
        centred = summed - jnp.mean(summed, axis=-1, keepdims=True)
        scale = lax.rsqrt(jnp.mean(centred * centred, axis=-1, keepdims=True) + 1e-05)
        nf = centred * scale
        for i in range(per):
            h = k * per + i
            inv[h] = jnp.broadcast_to(scale[i * piece : (i + 1) * piece], (piece, 128))
            normed_f[h] = nf[i * piece : (i + 1) * piece]
            normed[h] = nf[i * piece : (i + 1) * piece].astype(BF16)
            start(nrm_copies(h))
            normp[h, mine] = normed[h, mine]

    loads[0].wait()
    columns_of(strip * rows, rows)
    loads[1].wait()
    forward((rows + 1) * strip, rows - 1)
    loads[2].wait()
    norm(0)
    for h in range(per, chunks):
        start(cot_copies(h))
    mark("norm0")
    wait(near_copies(1))
    columns_of(first(1, other), block)
    forward(rows - 1, 2)
    norm(1)
    mark("norm1")
    wait(near_copies(0))
    columns_of(first(0, other), block)
    forward((rows + 1) * other, rows - 1)
    for item in loads[3:]:
        item.wait()
    for r in range(3):
        for c in range(3):
            w2t[r, pl.ds(c * chan, chan)] = w2[2 - r, pl.ds((2 - c) * chan, chan), :].T
    slope2[...] = silu_slope(hidden[...].astype(F32))
    mark("forward")

    ia = lax.rem(lax.broadcasted_iota(jnp.int32, (piece, piece), 0), share)
    ib = lax.rem(lax.broadcasted_iota(jnp.int32, (piece, piece), 1), share)
    same = ia == ib
    factor = chan ** (-0.5)

    def attend(h):
        rp = normp[h]
        query = dot(rp, wq[...]).astype(BF16)
        key = dot(rp, wk[...]).astype(BF16)
        value = dot(rp, wv[...]).astype(BF16)
        scores = jnp.where(same, dot_nt(query, key) * factor, -jnp.inf)
        expo = jnp.exp(scores - jnp.max(scores, axis=-1, keepdims=True))
        prob_f = expo / jnp.sum(expo, axis=-1, keepdims=True)
        prob = prob_f.astype(BF16)
        gm = dot_nt(cotp[h], wo[...]).astype(BF16)
        grad_prob = dot_nt(gm, value)
        inner = jnp.sum(prob_f * grad_prob, axis=-1, keepdims=True)
        grad_score = (prob_f * (grad_prob - inner) * factor).astype(BF16)
        grad_value = dot_tn(prob, gm).astype(BF16)
        grad_query = dot(grad_score, key).astype(BF16)
        grad_key = dot_tn(grad_score, query).astype(BF16)
        back = (
            dot_nt(grad_query, wq[...]) + dot_nt(grad_key, wk[...]) + dot_nt(grad_value, wv[...])
        )
        backp[h] = back.astype(BF16)
        start(bck_copies(h))
        gn[h, mine] = backp[h, mine]
        gq[h] = grad_query
        gk[h] = grad_key
        gv[h] = grad_value
        mx[h] = dot(prob, value).astype(BF16)

    for h in range(chunks):
        wait(cot_copies(h))
        cotp[h, mine] = cotv[from_cot(h, mine)]
        wait(nrm_copies(h))
        attend(h)
        mark("attend%d" % h)
    parts = part_a.shape[3]
    unit = chan // (views * parts)
    for t, (lhs, rhs) in enumerate(((normp, gq), (normp, gk), (normp, gv), (mx, cotp))):
        term = dot_tn(
            lhs[...].reshape(pixels, chan), rhs[...].reshape(pixels, chan)
        ).astype(BF16)
        for u in range(views * parts):
            v, q = divmod(u, parts)
            part_a[0, v // 2, v % 2, q, t] = term[u * unit : (u + 1) * unit]
    launch_a()
    step_a(1)
    mark("launch_a")

    def backward(h):
        row = start_row(h, strip)
        gnf = gn[h].astype(F32)
        nf = normed_f[h]
        gsum = cotv[span(row - strip * rows, each)].astype(F32) + inv[h, :, 0:1] * (
            gnf
            - jnp.mean(gnf, axis=-1, keepdims=True)
            - nf * jnp.mean(gnf * nf, axis=-1, keepdims=True)
        )
        gs[span(row - strip * rows, each)] = gsum
        g2[span(row, each)] = gsum.astype(BF16)
        start(swap_copies(h, 0))
        build(colsg, row + 1, g2[span(row, each)].astype(F32))

    for h in range(chunks):
        wait(bck_copies(h))
        backward(h)
    mark("backward")
    for r in range(3):
        acc[r] = dot_tn(
            cols2[span(strip * rows + r, rows)], g2[span(strip * rows, rows), columns]
        )
    for h in range(chunks):
        start(swap_copies(h, 1))

    def flipped(row, count):
        slope = conv(colsg, w2t, row, count)
        g1[span(row + 1, count)] = (slope * slope2[span(row, count)]).astype(BF16)

    flipped((rows + 1) * strip, rows - 1)
    for r in range(3):
        row = (rows + 1) * strip
        acc1[r] = dot_tn(cols1[span(row + r, rows - 1)], g1[span(row + 1, rows - 1), columns])
    for h in range(chunks):
        wait(swap_copies(h, 0))
    for r in range(3):
        term = dot_tn(cols2[span(other * rows + r, rows)], g2[span(other * rows, rows), columns])
        scatter(r, acc[r] + term, part_b)
    launch_b()
    step_b(1)
    mark("launch_b")
    for h in range(chunks):
        wait(swap_copies(h, 1))
        row = start_row(h, other)
        build(colsg, row + 1, g2[span(row, each)].astype(F32))
    mark("swapped")

    mark("g2all")
    flipped((rows - 1) * other, rows + 1)
    for r in range(3):
        row = (rows - 1) * other
        term = dot_tn(cols1[span(row + r, rows + 1)], g1[span(row + 1, rows + 1), columns])
        scatter(r, acc1[r] + term, part_c)
    launch_c()
    mark("launch_c")
    build(colsg, 0, g1[span(strip * rows, rows + 2)].astype(F32))
    step_c(1)
    step_a(2)
    slope = conv_flip(colsg, w1, 0, rows)
    gfeat[...] = (
        gs[...] + slope * silu_slope(fmap[span(strip * rows, rows)].astype(F32))
    ).astype(BF16)
    mark("gfeat")
    step_b(2)
    mark("step_b2")
    step_c(2)
    mark("step_c2")

    def store_a(u, value):
        attn_out[:, pl.ds(u * unit, unit), :] = value.astype(attn_out.dtype)

    def store_conv(i):
        def store(u, value):
            p, t = divmod(u, strips)
            size = value.shape[0]
            conv_out[i, pl.ds(p * size, size), pl.ds(t * lanes, lanes)] = value.astype(
                conv_out.dtype
            )

        return store

    finish_a(store_a)
    finish_b(store_conv(1))
    finish_c(store_conv(0))


def widen(a, b, c, x, y, z):
    x[...] = a[...]
    y[...] = b[...].astype(F32)
    z[...] = c[...].astype(F32)


def body(features, cotangent, conv_first, conv_second, w_query, w_key, w_value, w_out):
    views = lax.axis_size("view")
    strips = lax.axis_size("strip")
    _, rows, width, chan = features.shape
    pixels = rows * width
    zs = views // 2
    cut = 9 * chan // views
    slab = chan // views
    vm = pltpu.VMEM
    dma = pltpu.SemaphoreType.DMA
    flat = (pixels, chan)
    split = (CHUNKS, pixels // CHUNKS, chan)
    wide = (rows + 2 * DEEP) * width
    near = (rows + 2) * width
    exact = cut % (16 * strips) == 0 and slab % (16 * strips) == 0
    parts = strips if exact else 1
    pieces = 3 if cut % (48 * parts) == 0 else 1
    full = strips == 2 and exact and pieces == 3 and rows == 2 * DEEP and chan % 256 == 0
    conv_u = (cut // (parts * pieces), chan)
    attn_u = (4, slab // parts, chan)
    units = ((1, attn_u), (pieces, conv_u), (pieces, conv_u))
    total = 1 + 2 * pieces
    hold = {
        "part_": [(n, zs, 2, parts) + u for n, u in units],
        "r1": [(n, zs, parts) + u for n, u in units],
        "t1": [(n, parts, zs) + u for n, u in units],
        "r2": [(n, max(parts - 1, 1), zs) + u for n, u in units],
        "t2": [(n, zs) + u for n, u in units],
        "r3": [(n, zs - 1) + u for n, u in units],
        "r4": [(n, strips) + u for n, u in units],
    }
    conv_k = (3, 3 * chan, chan)
    square = (chan, chan)
    scratch = {
        "w1": vm(conv_k, BF16), "w2": vm(conv_k, BF16),
        "wq": vm(square, BF16), "wk": vm(square, BF16),
        "wv": vm(square, BF16), "wo": vm(square, BF16), "load": dma((9,)),
        "fmap": vm((wide, chan), BF16), "cotv": vm(split, BF16),
        "cols1": vm((wide, 3 * chan), BF16), "cols2": vm((near, 3 * chan), BF16),
        "colsg": vm((wide, 3 * chan), BF16),
        "hidden": vm((near, chan), BF16), "normed": vm(split, BF16), "normed_f": vm(split, F32),
        "inv": vm(split[:2] + (128,), F32), "g2": vm((wide, chan), BF16), "gs": vm(split, F32),
        "g1": vm((near, chan), BF16),
    }
    for name in ("normp", "cotp", "backp", "gn", "gq", "gk", "gv", "mx"):
        scratch[name] = vm(split, BF16)
    for name, shapes in hold.items():
        for letter, shape in zip("abc", shapes):
            scratch[name + letter] = vm(shape, BF16)
    if full:
        conv_u = (cut // pieces, chan // strips)
        attn_u = (4, slab, chan)
        scratch["part_a"] = vm((1, zs, 2, 1) + attn_u, BF16)
        scratch["r1a"] = vm((1, zs, 1) + attn_u, BF16)
        scratch["t2a"] = vm((1, zs) + attn_u, BF16)
        scratch["r3a"] = vm((1, zs - 1) + attn_u, BF16)
        scratch["r4a"] = vm((1, strips) + attn_u, BF16)
        del scratch["t1a"], scratch["r2a"]
        for letter in "bc":
            scratch["part_" + letter] = vm((pieces, zs, 2, 1) + conv_u, BF16)
            scratch["r1" + letter] = vm((pieces, zs, 1) + conv_u, BF16)
            scratch["t2" + letter] = vm((pieces, zs) + conv_u, BF16)
            scratch["r3" + letter] = vm((pieces, zs - 1) + conv_u, BF16)
            scratch["r4" + letter] = vm((pieces, strips) + conv_u, BF16)
            del scratch["t1" + letter], scratch["r2" + letter]
        padded = (strips * rows + 2) * width
        for name in ("cols1", "cols2", "colsg"):
            scratch[name] = vm((padded, 3 * chan), BF16)
        for name in ("fmap", "hidden", "g2"):
            scratch[name] = vm((strips * pixels, chan), BF16)
        scratch["g1"] = vm((padded, chan), BF16)
        parcels = PARCELS if rows % PARCELS == 0 and width * rows % (16 * views * PARCELS) == 0 else 2
        lots = (parcels, pixels // parcels, chan)
        for name in ("normp", "cotp", "backp", "gn", "gq", "gk", "gv", "mx", "normed"):
            scratch[name] = vm(lots, BF16)
        scratch["normed_f"] = vm(lots, F32)
        scratch["inv"] = vm(lots[:2] + (128,), F32)
        scratch["cotv"] = vm(flat, BF16)
        scratch["gs"] = vm(flat, F32)
        scratch["acc"] = scratch["acc1"] = vm((3, 3 * chan, chan // strips), F32)
        scratch["w2t"] = vm(conv_k, BF16)
        scratch["slope2"] = vm((strips * pixels, chan), F32)
    counts = {
        "halo": (2, 2), "cot": (views,), "nrm": (CHUNKS, views), "bck": (CHUNKS, views),
        "s1": (total,), "s2": (total, strips), "s3": (total, zs), "s4": (total, strips),
    }
    if full:
        del counts["halo"]
        counts["near"] = (2, SPLIT)
        counts["swap"] = (parcels, 2)
        counts["cot"] = counts["nrm"] = counts["bck"] = (parcels, views)
    for name, shape in counts.items():
        scratch[name + "_send"] = dma(shape)
        scratch[name + "_recv"] = dma(shape)
    names = (
        "feat", "cot", "w1h", "w2h", "wqh", "wkh", "wvh", "woh", "gfeat", "conv_out", "attn_out",
    ) + tuple(scratch)
    spec = pl.BlockSpec(memory_space=pltpu.VMEM)
    stay = pl.BlockSpec(memory_space=pl.ANY)
    kind = BF16 if exact else F32
    conv_s = (2, cut, chan)
    attn_s = (4, slab, chan)
    outs = pl.pallas_call(
        functools.partial(
            kernel, run_full if full else run, (views, strips, rows, width, chan), names
        ),
        out_shape=(
            jax.ShapeDtypeStruct(flat, BF16),
            jax.ShapeDtypeStruct(conv_s, kind),
            jax.ShapeDtypeStruct(attn_s, kind),
        ),
        in_specs=[stay] * 8,
        out_specs=(spec, spec, spec),
        scratch_shapes=list(scratch.values()),
        compiler_params=pltpu.CompilerParams(
            collective_id=0, has_side_effects=True, vmem_limit_bytes=48 * 1024 * 1024
        ),
    )(
        *[
            pltpu.with_memory_space_constraint(x, pltpu.HBM)
            for x in (
                features.reshape(flat),
                cotangent.reshape(flat if full else split),
                conv_first.reshape(3, 3 * chan, chan),
                conv_second.reshape(3, 3 * chan, chan),
                w_query, w_key, w_value, w_out,
            )
        ]
    )
    outs = pl.pallas_call(
        widen,
        out_shape=(
            jax.ShapeDtypeStruct(flat, BF16),
            jax.ShapeDtypeStruct(conv_s, F32),
            jax.ShapeDtypeStruct(attn_s, F32),
        ),
        in_specs=[spec] * 3,
        out_specs=(spec, spec, spec),
        compiler_params=pltpu.CompilerParams(vmem_limit_bytes=8 * 1024 * 1024),
    )(*outs)
    return (outs[0].reshape(features.shape), outs[1], outs[2])


def solution(mesh):
    rows = P(("orbit", "view"), "strip", None, None)
    grads = P("orbit", "view", None)
    return jax.shard_map(
        body,
        mesh=mesh,
        in_specs=(rows, rows, P(), P(), P(), P(), P(), P()),
        out_specs=(rows, grads, grads),
        check_vma=False,
    )
```

```python
import functools
import math

import jax
import jax.numpy as jnp
from jax import lax
from jax.experimental import pallas as pl
from jax.experimental.pallas import tpu as pltpu
from jax.sharding import PartitionSpec as P

MESH = pl.DeviceIdType.MESH
F32 = jnp.float32
BF16 = jnp.bfloat16
NT = (((1,), (1,)), ((), ()))
TN = (((0,), (0,)), ((), ()))
CHUNKS = 2
DEEP = 2
SPLIT = 1
PARCELS = 4


def dot(a, b):
    return jnp.dot(a, b, preferred_element_type=F32)


def dot_nt(a, b):
    return lax.dot_general(a, b, NT, preferred_element_type=F32)


def dot_tn(a, b):
    return lax.dot_general(a, b, TN, preferred_element_type=F32)


def silu(x):
    return x * jax.nn.sigmoid(x)


def silu_slope(x):
    sigma = jax.nn.sigmoid(x)
    return sigma * (1.0 + x * (1.0 - sigma))


def group(place, sems, start, wait, base, part, r1, t1, r2, t2, r3, r4, split=False):
    view, strip, core, zed, views, strips, zs = place
    s1_send, s1_recv, s2_send, s2_recv, s3_send, s3_recv, s4_send, s4_recv = sems
    parts = part.shape[3]
    shares = split or parts > 1

    def stage1(p):
        return [
            pltpu.make_async_remote_copy(
                src_ref=part.at[p, :, 1 - core], dst_ref=r1.at[p],
                send_sem=s1_send.at[base + p], recv_sem=s1_recv.at[base + p],
                device_id={"view": view + 1 - 2 * core}, device_id_type=MESH,
            )
        ]

    def reduce1(p):
        for j in range(zs):
            if t1 is None:
                t2[p, j] = (
                    part[p, j, core, 0].astype(F32) + r1[p, j, 0].astype(F32)
                ).astype(BF16)
                continue
            for t in range(parts):
                t1[p, t, j] = (
                    part[p, j, core, t].astype(F32) + r1[p, j, t].astype(F32)
                ).astype(BF16)

    def stage2(p):
        out = []
        for k in range(1, parts):
            other = lax.rem(strip + k, strips)
            out.append(
                pltpu.make_async_remote_copy(
                    src_ref=t1.at[p, other], dst_ref=r2.at[p, k - 1],
                    send_sem=s2_send.at[base + p, k], recv_sem=s2_recv.at[base + p, k],
                    device_id={"strip": other}, device_id_type=MESH,
                )
            )
        return out

    def reduce2(p):
        own = strip if parts > 1 else 0
        for j in range(zs):
            value = t1[p, own, j].astype(F32)
            for k in range(1, parts):
                value = value + r2[p, k - 1, j].astype(F32)
            t2[p, j] = value.astype(BF16)

    def stage3(p):
        out = []
        for k in range(1, zs):
            other = lax.rem(zed + k, zs)
            out.append(
                pltpu.make_async_remote_copy(
                    src_ref=t2.at[p, other], dst_ref=r3.at[p, k - 1],
                    send_sem=s3_send.at[base + p, k], recv_sem=s3_recv.at[base + p, k],
                    device_id={"view": other * 2 + core}, device_id_type=MESH,
                )
            )
        return out

    def reduce3(p):
        value = t2[p, zed].astype(F32)
        for k in range(1, zs):
            value = value + r3[p, k - 1].astype(F32)
        r4[p, strip] = value.astype(BF16)

    def stage4(p):
        out = []
        for k in range(1, strips):
            out.append(
                pltpu.make_async_remote_copy(
                    src_ref=r4.at[p, strip], dst_ref=r4.at[p, strip],
                    send_sem=s4_send.at[base + p, k], recv_sem=s4_recv.at[base + p, k],
                    device_id={"strip": lax.rem(strip + k, strips)}, device_id_type=MESH,
                )
            )
        return out

    def final(p):
        if shares:
            return [r4[p, t].astype(F32) for t in range(strips)]
        value = r4[p, 0].astype(F32)
        for t in range(1, strips):
            value = value + r4[p, t].astype(F32)
        return [value]

    reduces = (None, reduce1, reduce2, reduce3)
    stages = (stage1, stage2, stage3, stage4)
    if t1 is None:
        reduces = (None, reduce1, reduce3)
        stages = (stage1, stage3, stage4)

    def launch():
        for p in range(part.shape[0]):
            start(stage1(p))

    def advance(k, p):
        wait(stages[k - 1](p))
        reduces[k](p)
        start(stages[k](p))

    def advance_all(k):
        for p in range(part.shape[0]):
            advance(k, p)

    def finish(store):
        for p in range(part.shape[0]):
            wait(stage4(p))
            for t, value in enumerate(final(p)):
                store(p * (strips if shares else 1) + t, value)

    return launch, advance_all, finish


def mark(name):
    pass


def kernel(call, dims, names, *refs):
    call(dims, **dict(zip(names, refs, strict=True)))


def run(
    dims, feat, cot, w1h, w2h, wqh, wkh, wvh, woh, gfeat, conv_out, attn_out,
    w1, w2, wq, wk, wv, wo, load,
    fmap, cotv, cols1, cols2, colsg, hidden, normed, normed_f, inv, g2, gs, g1,
    normp, cotp, backp, gn, gq, gk, gv, mx,
    part_a, part_b, part_c, r1a, r1b, r1c, t1a, t1b, t1c, r2a, r2b, r2c,
    t2a, t2b, t2c, r3a, r3b, r3c, r4a, r4b, r4c,
    halo_send, halo_recv, cot_send, cot_recv, nrm_send, nrm_recv, bck_send, bck_recv,
    s1_send, s1_recv, s2_send, s2_recv, s3_send, s3_recv, s4_send, s4_recv,
):
    views, strips, rows, width, chan = dims
    pixels = rows * width
    half = pixels // CHUNKS
    share = half // views
    edge = DEEP * width
    zs = views // 2
    view = lax.axis_index("view")
    strip = lax.axis_index("strip")
    core = lax.rem(view, 2)
    zed = lax.div(view, 2)

    barrier = pltpu.get_barrier_semaphore()
    for k in range(1, views):
        pl.semaphore_signal(
            barrier, inc=1, device_id={"view": lax.rem(view + k, views)}, device_id_type=MESH
        )
    for k in range(1, strips):
        pl.semaphore_signal(
            barrier, inc=1, device_id={"strip": lax.rem(strip + k, strips)}, device_id_type=MESH
        )
    mine = pl.ds(pl.multiple_of(view * share, share), share)
    loads = [
        pltpu.make_async_copy(src, dst, load.at[i])
        for i, (src, dst) in enumerate(
            (
                (feat, fmap.at[pl.ds(edge, pixels)]),
                (w1h, w1), (w2h, w2), (woh, wo), (wqh, wq), (wkh, wk), (wvh, wv),
                (cot.at[:, mine], cotp.at[:, mine]), (cot, cotv),
            )
        )
    ]
    for item in loads:
        item.start()

    @pl.when(strip == 0)
    def _():
        fmap[pl.ds(0, edge)] = jnp.zeros((edge, chan), BF16)
        g2[pl.ds(0, edge)] = jnp.zeros((edge, chan), BF16)

    @pl.when(strip == strips - 1)
    def _():
        fmap[pl.ds(edge + pixels, edge)] = jnp.zeros((edge, chan), BF16)
        g2[pl.ds(edge + pixels, edge)] = jnp.zeros((edge, chan), BF16)

    pl.semaphore_wait(barrier, views - 1 + strips - 1)

    def halo_copy(e, src, dst, way):
        start = 0 if way == 0 else pixels - edge
        land = edge + pixels if way == 0 else 0
        near = lax.max(strip - 1, 0) if way == 0 else lax.min(strip + 1, strips - 1)
        base = edge if src is dst else 0
        return pltpu.make_async_remote_copy(
            src_ref=src.at[pl.ds(base + start, edge)], dst_ref=dst.at[pl.ds(land, edge)],
            send_sem=halo_send.at[e, way], recv_sem=halo_recv.at[e, way],
            device_id={"strip": near}, device_id_type=MESH,
        )

    def halo_start(e, src, dst, way):
        copy = halo_copy(e, src, dst, way)
        pl.when(strip > 0 if way == 0 else strip < strips - 1)(copy.start)

    def halo_sent(e, src, dst, way):
        copy = halo_copy(e, src, dst, way)
        pl.when(strip > 0 if way == 0 else strip < strips - 1)(copy.wait_send)

    def halo_here(e, src, dst, way):
        copy = halo_copy(e, src, dst, way)
        pl.when(strip < strips - 1 if way == 0 else strip > 0)(copy.wait_recv)

    def spread(src, dst, send, recv):
        out = []
        for k in range(1, views):
            peer = lax.rem(view + k, views)
            out.append(
                pltpu.make_async_remote_copy(
                    src_ref=src(pl.ds(pl.multiple_of(peer * share, share), share)),
                    dst_ref=dst(mine),
                    send_sem=send(k), recv_sem=recv(k),
                    device_id={"view": peer}, device_id_type=MESH,
                )
            )
        return out

    def start(copies):
        for copy in copies:
            copy.start()

    def wait(copies):
        for copy in copies:
            copy.wait()

    def build(cols, offset, x):
        count = x.shape[0]
        column = lax.rem(lax.broadcasted_iota(jnp.int32, (count, chan), 0), width)
        left = jnp.where(column == 0, 0.0, pltpu.roll(x, 1, 0))
        right = jnp.where(column == width - 1, 0.0, pltpu.roll(x, count - 1, 0))
        cols[pl.ds(offset, count), pl.ds(0, chan)] = left.astype(BF16)
        cols[pl.ds(offset, count), pl.ds(chan, chan)] = x.astype(BF16)
        cols[pl.ds(offset, count), pl.ds(2 * chan, chan)] = right.astype(BF16)

    def conv(cols, w, offset, count):
        total = None
        for r in range(3):
            term = dot(cols[pl.ds(offset + r * width, count), :], w[r])
            total = term if total is None else total + term
        return total

    def conv_flip(cols, w, offset, count):
        total = None
        for r in range(3):
            for s in range(3):
                term = dot_nt(
                    cols[pl.ds(offset + r * width, count), pl.ds(s * chan, chan)],
                    w[2 - r, pl.ds((2 - s) * chan, chan), :],
                )
                total = term if total is None else total + term
        return total

    def wgrad(cols, offset, d, out):
        pieces, _, _, parts, unit, _ = out.shape
        per = 3 * chan // unit
        for r in range(3):
            value = dot_tn(cols[pl.ds(offset + r * width, pixels), :], d).astype(BF16)
            for m in range(per):
                u = r * per + m
                v, rest = divmod(u, pieces * parts)
                p, t = divmod(rest, parts)
                out[p, v // 2, v % 2, t] = value[m * unit : (m + 1) * unit]

    def inside(x, first, last):
        if first:
            low = lax.broadcasted_iota(jnp.int32, x.shape, 0)
            x = jnp.where(jnp.logical_and(low < width, strip == 0), 0.0, x)
        if last:
            high = lax.broadcasted_iota(jnp.int32, x.shape, 0)
            gone = jnp.logical_and(high >= x.shape[0] - width, strip == strips - 1)
            x = jnp.where(gone, 0.0, x)
        return x

    sems = (s1_send, s1_recv, s2_send, s2_recv, s3_send, s3_recv, s4_send, s4_recv)
    place = (view, strip, core, zed, views, strips, zs)
    count_a = part_a.shape[0]
    count_b = part_b.shape[0]
    launch_a, step_a, finish_a = group(
        place, sems, start, wait, 0, part_a, r1a, t1a, r2a, t2a, r3a, r4a
    )
    launch_b, step_b, finish_b = group(
        place, sems, start, wait, count_a, part_b, r1b, t1b, r2b, t2b, r3b, r4b
    )
    launch_c, step_c, finish_c = group(
        place, sems, start, wait, count_a + count_b, part_c, r1c, t1c, r2c, t2c, r3c, r4c
    )

    halo_start(0, feat, fmap, 0)
    halo_start(0, feat, fmap, 1)
    cot_copies = spread(
        lambda s: cot.at[:, s], lambda s: cotp.at[:, s],
        lambda k: cot_send.at[k], lambda k: cot_recv.at[k],
    )
    start(cot_copies)

    def forward(row, count, first=False, last=False):
        out = conv(cols1, w1, row * width, count * width).astype(BF16)
        hidden[pl.ds(row * width, count * width)] = out
        act = silu(out.astype(F32)).astype(BF16).astype(F32)
        build(cols2, row * width, inside(act, first, last))

    def nrm_copies(h):
        return spread(
            lambda s: normed.at[h, s], lambda s: normp.at[h, s],
            lambda k: nrm_send.at[h, k], lambda k: nrm_recv.at[h, k],
        )

    def norm(h):
        offset = h * half
        x = fmap[pl.ds(edge + offset, half)].astype(F32)
        summed = (x + conv(cols2, w2, offset, half)).astype(BF16).astype(F32)
        centred = summed - jnp.mean(summed, axis=-1, keepdims=True)
        scale = lax.rsqrt(jnp.mean(centred * centred, axis=-1, keepdims=True) + 1e-05)
        inv[h] = jnp.broadcast_to(scale, (half, 128))
        nf = centred * scale
        normed_f[h] = nf
        normed[h] = nf.astype(BF16)
        start(nrm_copies(h))
        normp[h, mine] = normed[h, mine]

    loads[0].wait()
    build(cols1, edge, silu(fmap[pl.ds(edge, pixels)].astype(F32)))
    loads[1].wait()
    forward(DEEP, rows - DEEP)
    halo_here(0, feat, fmap, 1)
    build(cols1, 0, silu(fmap[pl.ds(0, edge)].astype(F32)))
    forward(0, DEEP, first=True)
    loads[2].wait()
    norm(0)
    halo_here(0, feat, fmap, 0)
    build(cols1, edge + pixels, silu(fmap[pl.ds(edge + pixels, edge)].astype(F32)))
    forward(rows, DEEP, last=True)
    norm(1)
    mark("normed")

    for item in loads[3:]:
        item.wait()
    wait(cot_copies)
    gmix = dot_nt(cotp[...].reshape(pixels, chan), wo[...]).astype(BF16)
    ia = lax.rem(lax.broadcasted_iota(jnp.int32, (half, half), 0), share)
    ib = lax.rem(lax.broadcasted_iota(jnp.int32, (half, half), 1), share)
    same = ia == ib
    factor = chan ** (-0.5)

    def bck_copies(h):
        return spread(
            lambda s: backp.at[h, s], lambda s: gn.at[h, s],
            lambda k: bck_send.at[h, k], lambda k: bck_recv.at[h, k],
        )

    def attend(h):
        rp = normp[h]
        gm = gmix[h * half : (h + 1) * half]
        query = dot(rp, wq[...]).astype(BF16)
        key = dot(rp, wk[...]).astype(BF16)
        value = dot(rp, wv[...]).astype(BF16)
        scores = jnp.where(same, dot_nt(query, key) * factor, -jnp.inf)
        expo = jnp.exp(scores - jnp.max(scores, axis=-1, keepdims=True))
        prob_f = expo / jnp.sum(expo, axis=-1, keepdims=True)
        prob = prob_f.astype(BF16)
        grad_prob = dot_nt(gm, value)
        inner = jnp.sum(prob_f * grad_prob, axis=-1, keepdims=True)
        grad_score = (prob_f * (grad_prob - inner) * factor).astype(BF16)
        grad_value = dot_tn(prob, gm).astype(BF16)
        grad_query = dot(grad_score, key).astype(BF16)
        grad_key = dot_tn(grad_score, query).astype(BF16)
        back = (
            dot_nt(grad_query, wq[...]) + dot_nt(grad_key, wk[...]) + dot_nt(grad_value, wv[...])
        )
        backp[h] = back.astype(BF16)
        start(bck_copies(h))
        gn[h, mine] = backp[h, mine]
        gq[h] = grad_query
        gk[h] = grad_key
        gv[h] = grad_value
        mx[h] = dot(prob, value).astype(BF16)

    for h in range(CHUNKS):
        wait(nrm_copies(h))
        attend(h)
    mark("attended")
    parts = part_a.shape[3]
    unit = chan // (views * parts)
    for t, (lhs, rhs) in enumerate(((normp, gq), (normp, gk), (normp, gv), (mx, cotp))):
        term = dot_tn(
            lhs[...].reshape(pixels, chan), rhs[...].reshape(pixels, chan)
        ).astype(BF16)
        for u in range(views * parts):
            v, q = divmod(u, parts)
            part_a[0, v // 2, v % 2, q, t] = term[u * unit : (u + 1) * unit]
    launch_a()

    def backward(h):
        gnf = gn[h].astype(F32)
        nf = normed_f[h]
        gsum = cotv[h].astype(F32) + inv[h, :, 0:1] * (
            gnf
            - jnp.mean(gnf, axis=-1, keepdims=True)
            - nf * jnp.mean(gnf * nf, axis=-1, keepdims=True)
        )
        gs[h] = gsum
        g2[pl.ds(edge + h * half, half)] = gsum.astype(BF16)

    step_a(1)
    for h in range(CHUNKS):
        wait(bck_copies(h))
        backward(h)
        if h == 0:
            halo_start(1, g2, g2, 0)
    halo_start(1, g2, g2, 1)
    mark("g2")
    wgrad(cols2, 0, g2[pl.ds(edge, pixels)], part_b)
    launch_b()
    build(colsg, edge, g2[pl.ds(edge, pixels)].astype(F32))
    step_a(2)
    step_b(1)

    def flipped(row, count, first=False, last=False):
        slope = conv_flip(colsg, w2, row * width, count * width)
        own = slope * silu_slope(hidden[pl.ds(row * width, count * width)].astype(F32))
        g1[pl.ds(row * width, count * width)] = inside(own, first, last).astype(BF16)

    halo_here(1, g2, g2, 1)
    build(colsg, 0, g2[pl.ds(0, edge)].astype(F32))
    halo_here(1, g2, g2, 0)
    build(colsg, edge + pixels, g2[pl.ds(edge + pixels, edge)].astype(F32))
    flipped(0, rows + 2, True, True)
    mark("g1")
    wgrad(cols1, width, g1[pl.ds(width, pixels)], part_c)
    launch_c()
    build(colsg, 0, g1[...].astype(F32))
    step_c(1)
    step_b(2)
    slope = conv_flip(colsg, w1, 0, pixels)
    gfeat[...] = (
        gs[...].reshape(pixels, chan)
        + slope * silu_slope(fmap[pl.ds(edge, pixels)].astype(F32))
    ).astype(BF16)
    step_a(3)
    step_c(2)
    step_b(3)
    step_c(3)

    for way in range(2):
        halo_sent(0, feat, fmap, way)
        halo_sent(1, g2, g2, way)

    def store_a(u, value):
        attn_out[:, pl.ds(u * unit, unit), :] = value.astype(attn_out.dtype)

    def store_conv(i):
        def store(u, value):
            size = value.shape[0]
            conv_out[i, pl.ds(u * size, size), :] = value.astype(conv_out.dtype)

        return store

    finish_a(store_a)
    finish_b(store_conv(1))
    finish_c(store_conv(0))


def run_full(
    dims, feat, cot, w1h, w2h, wqh, wkh, wvh, woh, gfeat, conv_out, attn_out,
    w1, w2, wq, wk, wv, wo, load,
    fmap, cotv, cols1, cols2, colsg, hidden, normed, normed_f, inv, g2, gs, g1, acc, acc1, w2t, slope2,
    normp, cotp, backp, gn, gq, gk, gv, mx,
    part_a, part_b, part_c, r1a, r1b, r1c,
    t2a, t2b, t2c, r3a, r3b, r3c, r4a, r4b, r4c,
    near_send, near_recv, swap_send, swap_recv,
    cot_send, cot_recv, nrm_send, nrm_recv, bck_send, bck_recv,
    s1_send, s1_recv, s2_send, s2_recv, s3_send, s3_recv, s4_send, s4_recv,
):
    views, strips, rows, width, chan = dims
    pixels = rows * width
    chunks = normp.shape[0]
    piece = pixels // chunks
    block = rows // 2
    each = rows // chunks
    per = chunks // 2
    share = piece // views
    every = strips * pixels
    lanes = chan // strips
    zs = views // 2
    view = lax.axis_index("view")
    strip = lax.axis_index("strip")
    core = lax.rem(view, 2)
    zed = lax.div(view, 2)
    other = 1 - strip
    mine = pl.ds(pl.multiple_of(view * share, share), share)
    columns = pl.ds(pl.multiple_of(strip * lanes, lanes), lanes)

    def span(row, count):
        return pl.ds(pl.multiple_of(row * width, width), count * width)

    barrier = pltpu.get_barrier_semaphore()
    for k in range(1, views):
        pl.semaphore_signal(
            barrier, inc=1, device_id={"view": lax.rem(view + k, views)}, device_id_type=MESH
        )
    pl.semaphore_signal(barrier, inc=1, device_id={"strip": other}, device_id_type=MESH)
    loads = [
        pltpu.make_async_copy(src, dst, load.at[i])
        for i, (src, dst) in enumerate(
            (
                (feat, fmap.at[span(strip * rows, rows)]),
                (w1h, w1), (w2h, w2), (woh, wo), (wqh, wq), (wkh, wk), (wvh, wv), (cot, cotv),
            )
        )
    ]
    for item in loads:
        item.start()
    for cols in (cols1, cols2, colsg):
        cols[pl.ds(0, width)] = jnp.zeros((width, 3 * chan), BF16)
        cols[pl.ds(width + every, width)] = jnp.zeros((width, 3 * chan), BF16)
    g1[pl.ds(0, width)] = jnp.zeros((width, chan), BF16)
    g1[pl.ds(width + every, width)] = jnp.zeros((width, chan), BF16)
    pl.semaphore_wait(barrier, views)

    def start(copies):
        for copy in copies:
            copy.start()

    def wait(copies):
        for copy in copies:
            copy.wait()

    def first(k, which):
        return which * (3 * block) if k == 0 else block * (1 + which)

    def start_row(h, which):
        return first(h // per, which) + (h % per) * each

    def near_copies(k):
        out = []
        row = first(k, strip)
        for i in range(SPLIT):
            size = block * width // SPLIT
            place = pl.ds(pl.multiple_of(row * width + i * size, size), size)
            inside = pl.ds(pl.multiple_of((row - strip * rows) * width + i * size, size), size)
            out.append(
                pltpu.make_async_remote_copy(
                    src_ref=feat.at[inside], dst_ref=fmap.at[place],
                    send_sem=near_send.at[k, i], recv_sem=near_recv.at[k, i],
                    device_id={"strip": other}, device_id_type=MESH,
                )
            )
        return out

    def swap_copies(h, part):
        place = span(start_row(h, strip), each)
        which = pl.ds(pl.multiple_of((strip if part else other) * lanes, lanes), lanes)
        return [
            pltpu.make_async_remote_copy(
                src_ref=g2.at[place, which], dst_ref=g2.at[place, which],
                send_sem=swap_send.at[h, part], recv_sem=swap_recv.at[h, part],
                device_id={"strip": other}, device_id_type=MESH,
            )
        ]

    def spread(src, dst, send, recv):
        out = []
        for k in range(1, views):
            peer = lax.rem(view + k, views)
            out.append(
                pltpu.make_async_remote_copy(
                    src_ref=src(pl.ds(pl.multiple_of(peer * share, share), share)),
                    dst_ref=dst(mine),
                    send_sem=send(k), recv_sem=recv(k),
                    device_id={"view": peer}, device_id_type=MESH,
                )
            )
        return out

    def from_cot(h, s):
        place = start_row(h, strip) - strip * rows
        return pl.ds(pl.multiple_of(place * width + s.start, share), share)

    def cot_copies(h):
        return spread(
            lambda s: cot.at[from_cot(h, s)], lambda s: cotp.at[h, s],
            lambda k: cot_send.at[h, k], lambda k: cot_recv.at[h, k],
        )

    def nrm_copies(h):
        return spread(
            lambda s: normed.at[h, s], lambda s: normp.at[h, s],
            lambda k: nrm_send.at[h, k], lambda k: nrm_recv.at[h, k],
        )

    def bck_copies(h):
        return spread(
            lambda s: backp.at[h, s], lambda s: gn.at[h, s],
            lambda k: bck_send.at[h, k], lambda k: bck_recv.at[h, k],
        )

    def build(cols, row, x):
        count = x.shape[0]
        place = span(row, count // width)
        column = lax.rem(lax.broadcasted_iota(jnp.int32, (count, chan), 0), width)
        left = jnp.where(column == 0, 0.0, pltpu.roll(x, 1, 0))
        right = jnp.where(column == width - 1, 0.0, pltpu.roll(x, count - 1, 0))
        cols[place, pl.ds(0, chan)] = left.astype(BF16)
        cols[place, pl.ds(chan, chan)] = x.astype(BF16)
        cols[place, pl.ds(2 * chan, chan)] = right.astype(BF16)

    def conv(cols, w, row, count):
        total = None
        for r in range(3):
            term = dot(cols[span(row + r, count), :], w[r])
            total = term if total is None else total + term
        return total

    def conv_flip(cols, w, row, count):
        total = None
        for r in range(3):
            for s in range(3):
                term = dot_nt(
                    cols[span(row + r, count), pl.ds(s * chan, chan)],
                    w[2 - r, pl.ds((2 - s) * chan, chan), :],
                )
                total = term if total is None else total + term
        return total

    def scatter(r, value, out):
        unit = out.shape[4]
        size = math.gcd(3 * chan, unit)
        for m in range(3 * chan // size):
            v, low = divmod(r * 3 * chan + m * size, unit)
            out[0, v // 2, v % 2, 0, pl.ds(low, size)] = value[m * size : (m + 1) * size].astype(
                BF16
            )

    sems = (s1_send, s1_recv, s2_send, s2_recv, s3_send, s3_recv, s4_send, s4_recv)
    place = (view, strip, core, zed, views, strips, zs)
    count_a = part_a.shape[0]
    count_b = part_b.shape[0]
    launch_a, step_a, finish_a = group(
        place, sems, start, wait, 0, part_a, r1a, None, None, t2a, r3a, r4a
    )
    launch_b, step_b, finish_b = group(
        place, sems, start, wait, count_a, part_b, r1b, None, None, t2b, r3b, r4b, True
    )
    launch_c, step_c, finish_c = group(
        place, sems, start, wait, count_a + count_b, part_c, r1c, None, None, t2c, r3c, r4c, True
    )

    for h in range(per):
        start(cot_copies(h))
    start(near_copies(1))
    start(near_copies(0))

    def forward(row, count):
        out = conv(cols1, w1, row, count).astype(BF16)
        hidden[span(row, count)] = out
        build(cols2, row + 1, silu(out.astype(F32)).astype(BF16).astype(F32))

    def columns_of(row, count):
        build(cols1, row + 1, silu(fmap[span(row, count)].astype(F32)))

    def norm(k):
        row = first(k, strip)
        x = fmap[span(row, block)].astype(F32)
        summed = (x + conv(cols2, w2, row, block)).astype(BF16).astype(F32)
        centred = summed - jnp.mean(summed, axis=-1, keepdims=True)
        scale = lax.rsqrt(jnp.mean(centred * centred, axis=-1, keepdims=True) + 1e-05)
        nf = centred * scale
        for i in range(per):
            h = k * per + i
            inv[h] = jnp.broadcast_to(scale[i * piece : (i + 1) * piece], (piece, 128))
            normed_f[h] = nf[i * piece : (i + 1) * piece]
            normed[h] = nf[i * piece : (i + 1) * piece].astype(BF16)
            start(nrm_copies(h))
            normp[h, mine] = normed[h, mine]

    loads[0].wait()
    columns_of(strip * rows, rows)
    loads[1].wait()
    forward((rows + 1) * strip, rows - 1)
    loads[2].wait()
    norm(0)
    for h in range(per, chunks):
        start(cot_copies(h))
    mark("norm0")
    wait(near_copies(1))
    columns_of(first(1, other), block)
    forward(rows - 1, 2)
    norm(1)
    mark("norm1")
    wait(near_copies(0))
    columns_of(first(0, other), block)
    forward((rows + 1) * other, rows - 1)
    for item in loads[3:]:
        item.wait()
    for r in range(3):
        for c in range(3):
            w2t[r, pl.ds(c * chan, chan)] = w2[2 - r, pl.ds((2 - c) * chan, chan), :].T
    slope2[...] = silu_slope(hidden[...].astype(F32))
    mark("forward")

    ia = lax.rem(lax.broadcasted_iota(jnp.int32, (piece, piece), 0), share)
    ib = lax.rem(lax.broadcasted_iota(jnp.int32, (piece, piece), 1), share)
    same = ia == ib
    factor = chan ** (-0.5)

    def attend(h):
        rp = normp[h]
        query = dot(rp, wq[...]).astype(BF16)
        key = dot(rp, wk[...]).astype(BF16)
        value = dot(rp, wv[...]).astype(BF16)
        scores = jnp.where(same, dot_nt(query, key) * factor, -jnp.inf)
        expo = jnp.exp(scores - jnp.max(scores, axis=-1, keepdims=True))
        prob_f = expo / jnp.sum(expo, axis=-1, keepdims=True)
        prob = prob_f.astype(BF16)
        gm = dot_nt(cotp[h], wo[...]).astype(BF16)
        grad_prob = dot_nt(gm, value)
        inner = jnp.sum(prob_f * grad_prob, axis=-1, keepdims=True)
        grad_score = (prob_f * (grad_prob - inner) * factor).astype(BF16)
        grad_value = dot_tn(prob, gm).astype(BF16)
        grad_query = dot(grad_score, key).astype(BF16)
        grad_key = dot_tn(grad_score, query).astype(BF16)
        back = (
            dot_nt(grad_query, wq[...]) + dot_nt(grad_key, wk[...]) + dot_nt(grad_value, wv[...])
        )
        backp[h] = back.astype(BF16)
        start(bck_copies(h))
        gn[h, mine] = backp[h, mine]
        gq[h] = grad_query
        gk[h] = grad_key
        gv[h] = grad_value
        mx[h] = dot(prob, value).astype(BF16)

    for h in range(chunks):
        wait(cot_copies(h))
        cotp[h, mine] = cotv[from_cot(h, mine)]
        wait(nrm_copies(h))
        attend(h)
        mark("attend%d" % h)
    parts = part_a.shape[3]
    unit = chan // (views * parts)
    for t, (lhs, rhs) in enumerate(((normp, gq), (normp, gk), (normp, gv), (mx, cotp))):
        term = dot_tn(
            lhs[...].reshape(pixels, chan), rhs[...].reshape(pixels, chan)
        ).astype(BF16)
        for u in range(views * parts):
            v, q = divmod(u, parts)
            part_a[0, v // 2, v % 2, q, t] = term[u * unit : (u + 1) * unit]
    launch_a()
    step_a(1)
    mark("launch_a")

    def backward(h):
        row = start_row(h, strip)
        gnf = gn[h].astype(F32)
        nf = normed_f[h]
        gsum = cotv[span(row - strip * rows, each)].astype(F32) + inv[h, :, 0:1] * (
            gnf
            - jnp.mean(gnf, axis=-1, keepdims=True)
            - nf * jnp.mean(gnf * nf, axis=-1, keepdims=True)
        )
        gs[span(row - strip * rows, each)] = gsum
        g2[span(row, each)] = gsum.astype(BF16)
        start(swap_copies(h, 0))
        build(colsg, row + 1, g2[span(row, each)].astype(F32))

    for h in range(chunks):
        wait(bck_copies(h))
        backward(h)
    mark("backward")
    for r in range(3):
        acc[r] = dot_tn(
            cols2[span(strip * rows + r, rows)], g2[span(strip * rows, rows), columns]
        )
    for h in range(chunks):
        start(swap_copies(h, 1))

    def flipped(row, count):
        slope = conv(colsg, w2t, row, count)
        g1[span(row + 1, count)] = (slope * slope2[span(row, count)]).astype(BF16)

    flipped((rows + 1) * strip, rows - 1)
    for r in range(3):
        row = (rows + 1) * strip
        acc1[r] = dot_tn(cols1[span(row + r, rows - 1)], g1[span(row + 1, rows - 1), columns])
    for h in range(chunks):
        wait(swap_copies(h, 0))
    for r in range(3):
        term = dot_tn(cols2[span(other * rows + r, rows)], g2[span(other * rows, rows), columns])
        scatter(r, acc[r] + term, part_b)
    launch_b()
    step_b(1)
    mark("launch_b")
    for h in range(chunks):
        wait(swap_copies(h, 1))
        row = start_row(h, other)
        build(colsg, row + 1, g2[span(row, each)].astype(F32))
    mark("swapped")

    mark("g2all")
    flipped((rows - 1) * other, rows + 1)
    for r in range(3):
        row = (rows - 1) * other
        term = dot_tn(cols1[span(row + r, rows + 1)], g1[span(row + 1, rows + 1), columns])
        scatter(r, acc1[r] + term, part_c)
    launch_c()
    mark("launch_c")
    build(colsg, 0, g1[span(strip * rows, rows + 2)].astype(F32))
    step_c(1)
    step_a(2)
    slope = conv_flip(colsg, w1, 0, rows)
    gfeat[...] = (
        gs[...] + slope * silu_slope(fmap[span(strip * rows, rows)].astype(F32))
    ).astype(BF16)
    mark("gfeat")
    step_b(2)
    mark("step_b2")
    step_c(2)
    mark("step_c2")

    def store_a(u, value):
        attn_out[:, pl.ds(u * unit, unit), :] = value.astype(attn_out.dtype)

    def store_conv(i):
        def store(u, value):
            p, t = divmod(u, strips)
            size = value.shape[0]
            conv_out[i, pl.ds(p * size, size), pl.ds(t * lanes, lanes)] = value.astype(
                conv_out.dtype
            )

        return store

    finish_a(store_a)
    finish_b(store_conv(1))
    finish_c(store_conv(0))


def widen(a, b, c, x, y, z):
    x[...] = a[...]
    y[...] = b[...].astype(F32)
    z[...] = c[...].astype(F32)


def body(features, cotangent, conv_first, conv_second, w_query, w_key, w_value, w_out):
    views = lax.axis_size("view")
    strips = lax.axis_size("strip")
    _, rows, width, chan = features.shape
    pixels = rows * width
    zs = views // 2
    cut = 9 * chan // views
    slab = chan // views
    vm = pltpu.VMEM
    dma = pltpu.SemaphoreType.DMA
    flat = (pixels, chan)
    split = (CHUNKS, pixels // CHUNKS, chan)
    wide = (rows + 2 * DEEP) * width
    near = (rows + 2) * width
    exact = cut % (16 * strips) == 0 and slab % (16 * strips) == 0
    parts = strips if exact else 1
    pieces = 3 if cut % (48 * parts) == 0 else 1
    full = strips == 2 and exact and pieces == 3 and rows == 2 * DEEP and chan % 256 == 0
    conv_u = (cut // (parts * pieces), chan)
    attn_u = (4, slab // parts, chan)
    units = ((1, attn_u), (pieces, conv_u), (pieces, conv_u))
    total = 1 + 2 * pieces
    hold = {
        "part_": [(n, zs, 2, parts) + u for n, u in units],
        "r1": [(n, zs, parts) + u for n, u in units],
        "t1": [(n, parts, zs) + u for n, u in units],
        "r2": [(n, max(parts - 1, 1), zs) + u for n, u in units],
        "t2": [(n, zs) + u for n, u in units],
        "r3": [(n, zs - 1) + u for n, u in units],
        "r4": [(n, strips) + u for n, u in units],
    }
    conv_k = (3, 3 * chan, chan)
    square = (chan, chan)
    scratch = {
        "w1": vm(conv_k, BF16), "w2": vm(conv_k, BF16),
        "wq": vm(square, BF16), "wk": vm(square, BF16),
        "wv": vm(square, BF16), "wo": vm(square, BF16), "load": dma((9,)),
        "fmap": vm((wide, chan), BF16), "cotv": vm(split, BF16),
        "cols1": vm((wide, 3 * chan), BF16), "cols2": vm((near, 3 * chan), BF16),
        "colsg": vm((wide, 3 * chan), BF16),
        "hidden": vm((near, chan), BF16), "normed": vm(split, BF16), "normed_f": vm(split, F32),
        "inv": vm(split[:2] + (128,), F32), "g2": vm((wide, chan), BF16), "gs": vm(split, F32),
        "g1": vm((near, chan), BF16),
    }
    for name in ("normp", "cotp", "backp", "gn", "gq", "gk", "gv", "mx"):
        scratch[name] = vm(split, BF16)
    for name, shapes in hold.items():
        for letter, shape in zip("abc", shapes):
            scratch[name + letter] = vm(shape, BF16)
    if full:
        pieces = 1
        total = 3
        conv_u = (cut // pieces, chan // strips)
        attn_u = (4, slab, chan)
        scratch["part_a"] = vm((1, zs, 2, 1) + attn_u, BF16)
        scratch["r1a"] = vm((1, zs, 1) + attn_u, BF16)
        scratch["t2a"] = vm((1, zs) + attn_u, BF16)
        scratch["r3a"] = vm((1, zs - 1) + attn_u, BF16)
        scratch["r4a"] = vm((1, strips) + attn_u, BF16)
        del scratch["t1a"], scratch["r2a"]
        for letter in "bc":
            scratch["part_" + letter] = vm((pieces, zs, 2, 1) + conv_u, BF16)
            scratch["r1" + letter] = vm((pieces, zs, 1) + conv_u, BF16)
            scratch["t2" + letter] = vm((pieces, zs) + conv_u, BF16)
            scratch["r3" + letter] = vm((pieces, zs - 1) + conv_u, BF16)
            scratch["r4" + letter] = vm((pieces, strips) + conv_u, BF16)
            del scratch["t1" + letter], scratch["r2" + letter]
        padded = (strips * rows + 2) * width
        for name in ("cols1", "cols2", "colsg"):
            scratch[name] = vm((padded, 3 * chan), BF16)
        for name in ("fmap", "hidden", "g2"):
            scratch[name] = vm((strips * pixels, chan), BF16)
        scratch["g1"] = vm((padded, chan), BF16)
        parcels = PARCELS if rows % PARCELS == 0 and width * rows % (16 * views * PARCELS) == 0 else 2
        lots = (parcels, pixels // parcels, chan)
        for name in ("normp", "cotp", "backp", "gn", "gq", "gk", "gv", "mx", "normed"):
            scratch[name] = vm(lots, BF16)
        scratch["normed_f"] = vm(lots, F32)
        scratch["inv"] = vm(lots[:2] + (128,), F32)
        scratch["cotv"] = vm(flat, BF16)
        scratch["gs"] = vm(flat, F32)
        scratch["acc"] = scratch["acc1"] = vm((3, 3 * chan, chan // strips), F32)
        scratch["w2t"] = vm(conv_k, BF16)
        scratch["slope2"] = vm((strips * pixels, chan), F32)
    counts = {
        "halo": (2, 2), "cot": (views,), "nrm": (CHUNKS, views), "bck": (CHUNKS, views),
        "s1": (total,), "s2": (total, strips), "s3": (total, zs), "s4": (total, strips),
    }
    if full:
        del counts["halo"]
        counts["near"] = (2, SPLIT)
        counts["swap"] = (parcels, 2)
        counts["cot"] = counts["nrm"] = counts["bck"] = (parcels, views)
    for name, shape in counts.items():
        scratch[name + "_send"] = dma(shape)
        scratch[name + "_recv"] = dma(shape)
    names = (
        "feat", "cot", "w1h", "w2h", "wqh", "wkh", "wvh", "woh", "gfeat", "conv_out", "attn_out",
    ) + tuple(scratch)
    spec = pl.BlockSpec(memory_space=pltpu.VMEM)
    stay = pl.BlockSpec(memory_space=pl.ANY)
    kind = BF16 if exact else F32
    conv_s = (2, cut, chan)
    attn_s = (4, slab, chan)
    outs = pl.pallas_call(
        functools.partial(
            kernel, run_full if full else run, (views, strips, rows, width, chan), names
        ),
        out_shape=(
            jax.ShapeDtypeStruct(flat, BF16),
            jax.ShapeDtypeStruct(conv_s, kind),
            jax.ShapeDtypeStruct(attn_s, kind),
        ),
        in_specs=[stay] * 8,
        out_specs=(spec, spec, spec),
        scratch_shapes=list(scratch.values()),
        compiler_params=pltpu.CompilerParams(
            collective_id=0, has_side_effects=True, vmem_limit_bytes=48 * 1024 * 1024
        ),
    )(
        *[
            pltpu.with_memory_space_constraint(x, pltpu.HBM)
            for x in (
                features.reshape(flat),
                cotangent.reshape(flat if full else split),
                conv_first.reshape(3, 3 * chan, chan),
                conv_second.reshape(3, 3 * chan, chan),
                w_query, w_key, w_value, w_out,
            )
        ]
    )
    outs = pl.pallas_call(
        widen,
        out_shape=(
            jax.ShapeDtypeStruct(flat, BF16),
            jax.ShapeDtypeStruct(conv_s, F32),
            jax.ShapeDtypeStruct(attn_s, F32),
        ),
        in_specs=[spec] * 3,
        out_specs=(spec, spec, spec),
        compiler_params=pltpu.CompilerParams(vmem_limit_bytes=8 * 1024 * 1024),
    )(*outs)
    return (outs[0].reshape(features.shape), outs[1], outs[2])


def solution(mesh):
    rows = P(("orbit", "view"), "strip", None, None)
    grads = P("orbit", "view", None)
    return jax.shard_map(
        body,
        mesh=mesh,
        in_specs=(rows, rows, P(), P(), P(), P(), P(), P()),
        out_specs=(rows, grads, grads),
        check_vma=False,
    )
```
